32 devices in a mesh: obs: 4 (over z), src: 8 (over y, x, core).
Axes of the slice: x: 2, y: 2, z: 4, core: 2. Of those that a mesh axis runs over, the one named last changes fastest.
Arguments:
- history: bfloat16 [3, 64, 64, 1536], P(None, ('obs', 'src')), may hold values from -6 to 6
- incident: bfloat16 [5, 64, 64, 1536], P(None, ('obs', 'src')), may hold values from -6 to 6
- proj_basis: bfloat16 [64, 64, 1536], P(('obs', 'src')), may hold values from -0.15625 to 0.15625
- expand_basis: bfloat16 [64, 64, 1536], P(('obs', 'src')), may hold values from -0.75 to 0.75
- near_inverse: bfloat16 [64, 1536, 1536], P(('obs', 'src')), may hold values from -0.15625 to 0.15625
- couplings: bfloat16 [2, 4096, 4, 8, 128], P(None, 'obs', None, 'src'), may hold values from -0.09375 to 0.09375
- lags: int32 [64, 4, 8, 2], P('obs', None, 'src'), may hold values from 0 to 2, as said below
Outputs:
- currents: bfloat16 [5, 64, 64, 1536], P(None, ('obs', 'src'))
The draws below stay inside these ranges and needn't reach their ends.
Inputs may be any that keep to these rules, and one draw needn't show every extreme that they name: lags[j, o, s, k] is the lag from source cluster j to observer cluster (o * 8 + s) * 2 + k. Entries are 0, 1 or 2, and the entry of every cluster with itself is 0.
All inputs are finite; a program needn't handle non-finite values.
Results may differ from the reference program's by a relative error of at most 0.025.
Values may be sent and summed in bfloat16 or wider, within the bound.
A program may use at most 192 MiB of HBM per device.

```python
import math
import jax
import jax.numpy as jnp
from jax import lax

CL_DEV = 2
B = 1536
R = 64
E = 64
STEPS = 5
TAPS = 2
HIST = 3
C = 64
N_OBS = 4
N_SRC = 8


def draw_lags(key, part):
    shape = (C, N_OBS, N_SRC, CL_DEV)
    raw_value = jax.random.randint(key, shape, 0, 8)
    lag_value = jnp.where(raw_value == 0, 0, jnp.where(raw_value <= 4, 1, 2))
    source = lax.broadcasted_iota(jnp.int32, shape, 0)
    observer = (lax.broadcasted_iota(jnp.int32, shape, 1) * N_SRC + lax.broadcasted_iota(jnp.int32, shape, 2)) * CL_DEV + lax.broadcasted_iota(jnp.int32, shape, 3)
    return jnp.where(source == observer, 0, lag_value).astype(jnp.int32)


def strengthened(array, stream_key, source, target, parts, factor):
    owner, partner = [(jnp.arange(array.shape[axis_at]) // (array.shape[axis_at] // parts)).reshape([-1 if axis == axis_at else 1 for axis in range(array.ndim)]) for axis_at in (source, target)]
    chosen = jax.random.permutation(stream_key, parts)[partner]
    strong = (owner == chosen) | (owner == (partner + parts // 2) % parts)
    return jnp.where(strong, factor * array, array)


def block_levels(rng, dims, shards, low, top_value):
    def one(position, blocks):
        draws = jax.random.uniform(jax.random.fold_in(jax.random.fold_in(rng, 6), position), (blocks,), jnp.float32, low / len(shards), top_value / len(shards))
        return jnp.repeat(jnp.exp(draws), dims[position] // blocks).reshape((-1,) + (1,) * (len(dims) - position - 1))

    factor_of = one(*shards[0])
    for cut in shards[1:]:
        factor_of = factor_of * one(*cut)
    return factor_of


def bell_draw(own_key, shape, spread, most, shards=(), kind=jnp.bfloat16):
    drawn = jax.random.normal(own_key, shape, jnp.float32) * spread
    if len(shards) > 0:
        drawn = block_levels(own_key, shape, shards, -0.22, 0.18) * drawn
    return jnp.clip(drawn, min=-most, max=most).astype(kind)


def heavy_noise(key, shape, scale, limit, shards, heavy, held_as=jnp.bfloat16):
    drawn = scale * jax.random.normal(key, shape, jnp.float32)
    if shards:
        drawn = drawn * block_levels(key, shape, shards, -0.22, 0.18)
    return jnp.clip(strengthened(drawn, jax.random.fold_in(key, 3), *heavy), -limit, limit).astype(held_as)


def setup_inputs(seed: int = 0) -> dict:
    seeds = jax.random.split(jax.random.key(seed), 8)
    history = bell_draw(seeds[0], (HIST, C, E, B), 1.0, 6.0, ((1, 32),))
    incident = bell_draw(seeds[1], (STEPS, C, E, B), 1.0, 6.0, ((1, 32),))
    proj_basis = bell_draw(seeds[2], (C, R, B), B ** -0.5, 0.15625, ((0, 32),))
    expand_basis = bell_draw(seeds[3], (C, R, B), R ** -0.5, 0.75, ((0, 32),))
    near_inverse = bell_draw(seeds[4], (C, B, B), B ** -0.5, 0.15625, ((0, 32),))
    couplings = heavy_noise(seeds[5], (TAPS, C * R, N_OBS, N_SRC, CL_DEV * R), (2 * C * R) ** -0.5, 0.09375, ((1, 4), (3, 8)), (1, 2, 4, 2.0))
    lags = draw_lags(jax.random.fold_in(seeds[7], 71), 0)
    return dict(history=history, incident=incident, proj_basis=proj_basis, expand_basis=expand_basis, near_inverse=near_inverse, couplings=couplings, lags=lags)


def project(current, proj_basis):
    projected = jnp.einsum('ceb,crb->ecr', current.astype(jnp.float32), proj_basis.astype(jnp.float32), precision=lax.Precision.HIGHEST)
    return projected.astype(jnp.bfloat16).reshape(E, C * R)


def far_sum(stacked, kernel, lag_pairs):
    group_size = math.gcd(C, 16)
    block_count = C // group_size

    def one_block(block_index):
        start = (block_index * group_size).astype(jnp.int32)
        block_kernel = lax.dynamic_slice_in_dim(kernel, (start * R).astype(jnp.int32), group_size * R, 2)
        block_kernel = block_kernel.reshape(TAPS, C, R, group_size, R)
        block_lags = lax.dynamic_slice_in_dim(lag_pairs, start, group_size, 1)
        total = jnp.zeros((E, group_size * R), jnp.float32)
        for delay in range(1, HIST + 1):
            combined = jnp.zeros((C, R, group_size, R), jnp.bfloat16)
            for tap_index in range(TAPS):
                if delay - tap_index >= 1:
                    chosen = (block_lags == delay - tap_index)[:, None, :, None]
                    combined = jnp.where(chosen, block_kernel[tap_index], combined)
            total = total + jnp.dot(stacked[delay - 1], combined.reshape(C * R, group_size * R).astype(jnp.float32), precision=lax.Precision.HIGHEST)
        return total

    blocks = lax.map(one_block, jnp.arange(block_count, dtype=jnp.int32))
    return jnp.transpose(blocks, (1, 0, 2)).reshape(E, C * R)


def reference(history, incident, proj_basis, expand_basis, near_inverse, couplings, lags):
    kernel = couplings.reshape(TAPS, C * R, C * R)
    lag_pairs = lags.reshape(C, C)
    past = [project(history[slot_index], proj_basis) for slot_index in range(HIST)]
    results = []
    for step in range(STEPS):
        stacked = jnp.stack([past[len(past) - delay] for delay in range(1, HIST + 1)]).astype(jnp.float32)
        field = far_sum(stacked, kernel, lag_pairs).astype(jnp.bfloat16).reshape(E, C, R)
        far_field = jnp.einsum('ecr,crb->ceb', field.astype(jnp.float32), expand_basis.astype(jnp.float32), precision=lax.Precision.HIGHEST)
        residual_field = (incident[step].astype(jnp.float32) - far_field).astype(jnp.bfloat16)

        def near_apply(pair):
            return jnp.dot(pair[0].astype(jnp.float32), pair[1].astype(jnp.float32), precision=lax.Precision.HIGHEST)

        current = lax.map(near_apply, (residual_field, near_inverse)).astype(jnp.bfloat16)
        results.append(current)
        past.append(project(current, proj_basis))
    return jnp.stack(results)
```

```python
import contextlib
import functools

import jax
import jax.numpy as jnp
from jax import lax
from jax.experimental import pallas as pl
from jax.experimental.pallas import tpu as pltpu
from jax.sharding import PartitionSpec as P

MESH = pl.DeviceIdType.MESH
F32 = jnp.float32
BF16 = jnp.bfloat16
NT = (((1,), (1,)), ((), ()))
VMEM_LIMIT = 60000 * 1024


def scope(name):
    return contextlib.nullcontext()


def flipped(me, bits, count):
    other = me
    place = 1
    while place < count:
        if bits & place:
            other = other + (1 - 2 * ((me // place) % 2)) * place
        place *= 2
    return other


def partner(me, turn, count):
    if count & (count - 1) == 0:
        return flipped(me, count - turn, count)
    return lax.rem(me + turn, count)


def farthest_first(me, count):
    upper = (2 * me) // count
    sign = 1 - 2 * upper
    near_end = me * (1 - upper) + (count - 1 - me) * upper
    peers = []
    for i in range(count - 1):
        one_sided = (3 * count - 2 - i - 2 * near_end) // (2 * count)
        left = count - 2 - i
        paired = (left // 2 + 1) * (2 * (left % 2) - 1)
        peers.append(me + sign * (one_sided * (count - 1 - near_end - i) + (1 - one_sided) * paired))
    return peers


def kernel(n_obs, n_src, hist_ref, inc_ref, proj_ref, expand_ref, near_ref, coup_ref, lag_ref, out_ref,
           hv, av, pv, nv, cv, cf, wv, yv, xn, bv, mv, qh, qn, sendp, recvp, base,
           h_sem, a_sem, c_sem, n_sem, hs_sem, hr_sem, hf_sem, qs_sem, qr_sem, ps_sem, pr_sem):
    o = lax.axis_index("obs")
    s = lax.axis_index("src")
    hist, clusters, excite, unknowns = hist_ref.shape
    steps = inc_ref.shape[0]
    rank = proj_ref.shape[1]
    width = clusters * rank
    sources = lag_ref.shape[2]
    tile = 512
    tiles = unknowns // tile
    pairs = n_src // 2
    deep = 2 * width

    def rows(index, size):
        return pl.ds(index * size, size)

    def cols(index, size):
        return slice(index * size, (index + 1) * size)

    def local(src, dst, sem):
        pltpu.make_async_copy(src, dst, sem).start()

    def landed(ref, sem):
        pltpu.make_async_copy(ref, ref, sem).wait()

    for c in range(clusters):
        local(proj_ref.at[c], pv.at[c, rows(c, rank)], h_sem.at[0])
    for k in range(hist):
        local(hist_ref.at[k], hv.at[k], h_sem.at[1])

    mine = s % 2
    own = s // 2
    sibling = s + 1 - 2 * mine
    others = [partner(own, turn, pairs) for turn in range(1, pairs)]
    arriving = [partner(own, turn, pairs) for turn in range(pairs - 1, 0, -1)]
    q_peers = [pair * 2 + core for pair in others for core in range(2)] + [sibling]
    p_peers = farthest_first(o, n_obs)

    barrier = pltpu.get_barrier_semaphore()
    for peer in q_peers:
        pl.semaphore_signal(barrier, inc=1, device_id=(o, peer), device_id_type=MESH)
    for peer in p_peers:
        pl.semaphore_signal(barrier, inc=1, device_id=(peer, s), device_id_type=MESH)

    local(coup_ref, cv, c_sem.at[0])

    def near_loads(c):
        for t in range(steps):
            local(inc_ref.at[t, c], av.at[c, rows(t, excite)], a_sem.at[c])
        local(expand_ref.at[c], av.at[c, rows(steps, excite)], a_sem.at[c])
        for j in range(tiles):
            local(near_ref.at[c, :, cols(j, tile)], nv.at[c, :, cols(j, tile)], n_sem.at[c, j])

    near_loads(0)

    for c in range(clusters):
        for k in range(clusters):
            if k != c:
                pv[c, cols(k, rank)] = jnp.zeros((rank, unknowns), BF16)
                xn[c, cols(k, rank)] = jnp.zeros((rank, unknowns), BF16)

    with scope("hload"):
        landed(proj_ref, h_sem.at[0])
        landed(hist_ref, h_sem.at[1])

    for c in range(1, clusters):
        near_loads(c)

    with scope("project"):
        past = jnp.zeros((hist * excite, width), F32)
        for c in range(clusters):
            past = past + lax.dot_general(
                hv[:, c].reshape(hist * excite, unknowns), pv[c], NT, preferred_element_type=F32)
        qh[s] = past.astype(BF16).reshape(hist, excite, width)
    with scope("barrier"):
        pl.semaphore_wait(barrier, n_src + n_obs - 2)

    def remote(src, dst, send_sem, recv_sem, device):
        return pltpu.make_async_remote_copy(
            src_ref=src, dst_ref=dst, send_sem=send_sem, recv_sem=recv_sem, device_id=device, device_id_type=MESH)

    def arrived(ref, sem):
        remote(ref, ref, hs_sem.at[0], sem, (o, sibling)).wait_recv()

    def sent(ref, sem):
        remote(ref, ref, sem, hr_sem.at[0, 0], (o, sibling)).wait_send()

    for k in range(hist):
        for pair in others:
            remote(qh.at[s, k], qh.at[s, k], hs_sem.at[0], hr_sem.at[own, k], (o, pair * 2 + mine)).start()
    remote(qh.at[s], qh.at[s], hs_sem.at[0], hf_sem.at[own], (o, sibling)).start()

    def forward(pair):
        slot = pair * 2 + mine
        for k in range(hist):
            arrived(qh.at[slot, k], hr_sem.at[pair, k])
            remote(qh.at[slot, k], qh.at[slot, k], hs_sem.at[0], hf_sem.at[pair], (o, sibling)).start()

    with scope("cload"):
        landed(coup_ref, c_sem.at[0])
    lane = lax.broadcasted_iota(jnp.int32, (rank, width), 1)

    def build(j, carry):
        for p in range(2):
            cf[p] = cv[p, pl.ds(pl.multiple_of(j * (rank * n_obs), rank * n_obs), rank * n_obs), :].astype(F32)
        at = pl.ds(pl.multiple_of(j * rank, rank), rank)
        for to in range(n_obs):
            lag = jnp.full((rank, width), lag_ref[to, 0, j], jnp.int32)
            for k in range(1, clusters):
                lag = jnp.where(lane >= k * rank, lag_ref[to, k, j], lag)
            first = cf[0, pl.ds(to, rank, stride=n_obs), :]
            second = cf[1, pl.ds(to, rank, stride=n_obs), :]
            zero = jnp.zeros_like(first)
            one, two = lag == 1, lag == 2
            wv[0, at, cols(to, width)] = jnp.where(one, first, zero).astype(BF16)
            wv[1, at, cols(to, width)] = jnp.where(two, first, jnp.where(one, second, zero)).astype(BF16)
            wv[2, at, cols(to, width)] = jnp.where(two, second, zero).astype(BF16)
        return carry

    with scope("build"):
        lax.fori_loop(0, sources, build, 0)

    def near_tile(c, j):
        at = cols(j, tile)
        if j == 0:
            landed(av.at[c], a_sem.at[c])
        landed(nv.at[c, :, at], n_sem.at[c, j])
        value = jnp.dot(av[c], nv[c, :, at], preferred_element_type=F32)
        yv[c, :, at] = value
        xn[c, cols(c, rank), at] = value[steps * excite:].astype(BF16)

    def near_end(c):
        value = lax.dot_general(yv[c].astype(BF16), pv[c], NT, preferred_element_type=F32)
        if c == 0:
            bv[...] = value[:steps * excite]
        else:
            bv[...] += value[:steps * excite]
        mv[cols(c, rank)] = value[steps * excite:].astype(BF16)

    for j in range(tiles):
        with scope(f"near0_{j}"):
            near_tile(0, j)
    for pair in arriving:
        with scope("forward"):
            forward(pair)
    with scope("nearend0"):
        near_end(0)

    def rows_of(pair):
        return pl.ds(pl.multiple_of(pair * deep, deep), deep)

    def both(get, pair):
        return jnp.concatenate([get(pair * 2 + core) for core in range(2)], axis=1)

    def send_partial(step, total):
        for to in range(n_obs):
            sendp[step * n_obs + to] = total[:, cols(to, width)].astype(BF16)
        for peer in p_peers:
            remote(sendp.at[step * n_obs + peer], recvp.at[step * n_obs + o], ps_sem.at[0], pr_sem.at[step % 2],
                   (peer, s)).start()

    total = jnp.zeros((excite, n_obs * width), F32)
    for pair in [own] + arriving:
        with scope("hwait"):
            arrived(qh.at[0], hf_sem.at[pair])
        with scope("first"):
            for d in range(1, hist + 1):
                part = both(lambda slot: qh[slot, hist - d], pair)
                total = total + jnp.dot(part, wv[d - 1, rows_of(pair), :], preferred_element_type=F32)
    with scope("sendp"):
        send_partial(0, total)

    for c in range(1, clusters):
        for j in range(tiles):
            with scope(f"near{c}_{j}"):
                near_tile(c, j)
        with scope(f"nearend{c}"):
            near_end(c)

    def slot_of(k):
        return jnp.concatenate([qh[j, k] for j in range(n_src)], axis=1)

    with scope("hbase"):
        for ahead in range(1, hist):
            total = None
            for d in range(ahead + 1, hist + 1):
                term = jnp.dot(slot_of(hist + ahead - d), wv[d - 1], preferred_element_type=F32)
                total = term if total is None else total + term
            base[ahead] = total
        for ahead in range(hist, steps):
            base[ahead] = jnp.zeros((excite, n_obs * width), F32)

    def newest_term(step, total):
        for place, pair in enumerate([own] + arriving):
            with scope(f"waitq{step}"):
                ready = qn.at[pl.ds(step * n_src + pair * 2, 2)] if place else qn.at[step * n_src + sibling]
                arrived(ready, qr_sem.at[step % 2, pair])
            part = both(lambda slot: qn[step * n_src + slot], pair)
            total = total + jnp.dot(part, wv[0, rows_of(pair), :], preferred_element_type=F32)
        return total

    def finish(step, field):
        for c in range(clusters):
            far = jnp.dot(field, xn[c], preferred_element_type=F32)
            out_ref[step, c] = (yv[c, cols(step, excite)] - far).astype(BF16)

    for step in range(steps):
        field = sendp[step * n_obs + o].astype(F32)
        with scope(f"waitp{step}"):
            arrived(recvp.at[pl.ds(0, n_obs - 1)], pr_sem.at[step % 2])
        for peer in p_peers:
            field = field + recvp[step * n_obs + peer].astype(F32)
        field = field.astype(BF16)
        if step + 1 == steps:
            with scope(f"finish{step}"):
                finish(step, field)
            break
        newest = bv[cols(step, excite)] - jnp.dot(field, mv[...], preferred_element_type=F32)
        qn[step * n_src + s] = newest.astype(BF16)
        for peer in q_peers:
            remote(qn.at[step * n_src + s], qn.at[step * n_src + s], qs_sem.at[0], qr_sem.at[step % 2, own],
                   (o, peer)).start()
        with scope(f"finish{step}"):
            finish(step, field)
        with scope(f"newest{step}"):
            total = newest_term(step, base[step + 1])
        send_partial(step + 1, total)
        with scope(f"base{step}"):
            columns = jnp.concatenate([qn[step * n_src + j] for j in range(n_src)], axis=1)
            for d in range(2, hist + 1):
                if step + d < steps:
                    base[step + d] += jnp.dot(columns, wv[d - 1], preferred_element_type=F32)

    with scope("sent"):
        sent(qh.at[pl.ds(0, n_src - 1)], hs_sem.at[0])
        sent(qn.at[pl.ds(0, (steps - 1) * (n_src - 1))], qs_sem.at[0])
        sent(sendp.at[pl.ds(0, steps * (n_obs - 1))], ps_sem.at[0])


def hand_on(made_ref, out_ref, sem):
    for t in range(made_ref.shape[0]):
        pltpu.make_async_copy(made_ref.at[t], out_ref.at[t], sem.at[0]).start()
    pltpu.make_async_copy(made_ref, out_ref, sem.at[0]).wait()


def per_device(n_obs, n_src, history, incident, proj_basis, expand_basis, near_inverse, couplings, lags):
    hist, clusters, excite, unknowns = history.shape
    steps = incident.shape[0]
    rank = proj_basis.shape[1]
    width = clusters * rank
    taps, src_rows = couplings.shape[:2]
    sources = lags.shape[0]
    obs_cols = n_obs * width
    pairs = n_src // 2
    flat = couplings.reshape(taps, src_rows * n_obs, width)
    lag_table = jnp.transpose(lags.reshape(sources, n_obs, clusters), (1, 2, 0))
    stacked = (steps + 1) * excite
    any_spec = pl.BlockSpec(memory_space=pl.ANY)
    vmem_spec = pl.BlockSpec(memory_space=pltpu.VMEM)
    dma = pltpu.SemaphoreType.DMA
    made = pl.pallas_call(
        functools.partial(kernel, n_obs, n_src),
        out_shape=pltpu.VMEM(incident.shape, BF16),
        in_specs=[any_spec] * 6 + [pl.BlockSpec(memory_space=pltpu.SMEM)],
        out_specs=vmem_spec,
        scratch_shapes=[
            pltpu.VMEM((hist, clusters, excite, unknowns), BF16),
            pltpu.VMEM((clusters, stacked, unknowns), BF16),
            pltpu.VMEM((clusters, width, unknowns), BF16),
            pltpu.VMEM((clusters, unknowns, unknowns), BF16),
            pltpu.VMEM((taps, src_rows * n_obs, width), BF16),
            pltpu.VMEM((taps, rank * n_obs, width), F32),
            pltpu.VMEM((hist, src_rows, obs_cols), BF16),
            pltpu.VMEM((clusters, stacked, unknowns), F32),
            pltpu.VMEM((clusters, width, unknowns), BF16),
            pltpu.VMEM((steps * excite, width), F32),
            pltpu.VMEM((width, width), BF16),
            pltpu.VMEM((n_src, hist, excite, width), BF16),
            pltpu.VMEM(((steps - 1) * n_src, excite, width), BF16),
            pltpu.VMEM((steps * n_obs, excite, width), BF16),
            pltpu.VMEM((steps * n_obs, excite, width), BF16),
            pltpu.VMEM((steps, excite, obs_cols), F32),
            dma((2,)),
            dma((clusters,)),
            dma((1,)),
            dma((clusters, unknowns // 512)),
            dma((1,)),
            dma((pairs, hist)),
            dma((pairs,)),
            dma((1,)),
            dma((2, pairs)),
            dma((1,)),
            dma((2,)),
        ],
        compiler_params=pltpu.CompilerParams(
            collective_id=0, has_side_effects=True, vmem_limit_bytes=VMEM_LIMIT
        ),
    )(history, incident, proj_basis, expand_basis, near_inverse, flat, lag_table)
    return pl.pallas_call(
        hand_on,
        out_shape=jax.ShapeDtypeStruct(incident.shape, BF16),
        in_specs=[vmem_spec],
        out_specs=any_spec,
        scratch_shapes=[dma((1,))],
        compiler_params=pltpu.CompilerParams(vmem_limit_bytes=8000 * 1024),
    )(made)


def solution(mesh):
    placed = (
        P(None, ("obs", "src"), None, None),
        P(None, ("obs", "src"), None, None),
        P(("obs", "src"), None, None),
        P(("obs", "src"), None, None),
        P(("obs", "src"), None, None),
        P(None, "obs", None, "src", None),
        P("obs", None, "src", None),
    )
    return jax.shard_map(
        functools.partial(per_device, mesh.shape["obs"], mesh.shape["src"]),
        mesh=mesh,
        in_specs=placed,
        out_specs=P(None, ("obs", "src"), None, None),
        check_vma=False,
    )
```

```python
import contextlib
import functools

import jax
import jax.numpy as jnp
from jax import lax
from jax.experimental import pallas as pl
from jax.experimental.pallas import tpu as pltpu
from jax.sharding import PartitionSpec as P

MESH = pl.DeviceIdType.MESH
F32 = jnp.float32
BF16 = jnp.bfloat16
NT = (((1,), (1,)), ((), ()))
VMEM_LIMIT = 60000 * 1024


def scope(name):
    return contextlib.nullcontext()


def flipped(me, bits, count):
    other = me
    place = 1
    while place < count:
        if bits & place:
            other = other + (1 - 2 * ((me // place) % 2)) * place
        place *= 2
    return other


def partner(me, turn, count):
    if count & (count - 1) == 0:
        return flipped(me, count - turn, count)
    return lax.rem(me + turn, count)


def farthest_first(me, count):
    upper = (2 * me) // count
    sign = 1 - 2 * upper
    near_end = me * (1 - upper) + (count - 1 - me) * upper
    peers = []
    for i in range(count - 1):
        one_sided = (3 * count - 2 - i - 2 * near_end) // (2 * count)
        left = count - 2 - i
        paired = (left // 2 + 1) * (2 * (left % 2) - 1)
        peers.append(me + sign * (one_sided * (count - 1 - near_end - i) + (1 - one_sided) * paired))
    return peers


def kernel(n_obs, n_src, hist_ref, inc_ref, proj_ref, expand_ref, near_ref, coup_ref, lags_ref, out_ref,
           lag_ref, hv, av, pv, nv, cv, cf, wv, yv, xn, bv, mv, qh, qn, sendp, recvp, base,
           l_sem, h_sem, a_sem, c_sem, n_sem, hs_sem, hr_sem, hf_sem, qs_sem, qr_sem, ps_sem, pr_sem):
    o = lax.axis_index("obs")
    s = lax.axis_index("src")
    hist, clusters, excite, unknowns = hist_ref.shape
    steps = inc_ref.shape[0]
    rank = proj_ref.shape[1]
    width = clusters * rank
    sources = lag_ref.shape[2]
    tile = 512
    tiles = unknowns // tile
    pairs = n_src // 2
    deep = 2 * width

    soon = min(2, steps)
    early = (soon + 1) * excite

    def place(step):
        return step if step < soon else step + 1

    def rows(index, size):
        return pl.ds(index * size, size)

    def cols(index, size):
        return slice(index * size, (index + 1) * size)

    def local(src, dst, sem):
        pltpu.make_async_copy(src, dst, sem).start()

    def landed(ref, sem):
        pltpu.make_async_copy(ref, ref, sem).wait()

    for c in range(clusters):
        local(proj_ref.at[c], pv.at[c, rows(c, rank)], h_sem.at[hist])
    for k in range(hist):
        for c in range(clusters):
            local(hist_ref.at[k, c], hv.at[k, c], h_sem.at[k])

    mine = s % 2
    own = s // 2
    sibling = s + 1 - 2 * mine
    others = [partner(own, turn, pairs) for turn in range(1, pairs)]
    arriving = [partner(own, turn, pairs) for turn in range(pairs - 1, 0, -1)]
    q_peers = [pair * 2 + core for pair in others for core in range(2)] + [sibling]
    p_peers = farthest_first(o, n_obs)

    barrier = pltpu.get_barrier_semaphore()
    for peer in q_peers:
        pl.semaphore_signal(barrier, inc=1, device_id=(o, peer), device_id_type=MESH)
    for peer in p_peers:
        pl.semaphore_signal(barrier, inc=1, device_id=(peer, s), device_id_type=MESH)

    local(lags_ref, lag_ref, l_sem.at[0])
    quarter = coup_ref.shape[1] // 4
    for p in range(coup_ref.shape[0]):
        for part in range(4):
            local(coup_ref.at[p, rows(part, quarter)], cv.at[p, rows(part, quarter)], c_sem.at[0])


    def stack_loads(c, part):
        for t in range(soon) if part == 0 else range(soon, steps):
            local(inc_ref.at[t, c], av.at[c, rows(place(t), excite)], a_sem.at[c, part])
        if part == 0:
            local(expand_ref.at[c], av.at[c, rows(soon, excite)], a_sem.at[c, part])

    def near_load(c, j):
        local(near_ref.at[c, :, cols(j, tile)], nv.at[c, :, cols(j, tile)], n_sem.at[c, j])


    def remote(src, dst, send_sem, recv_sem, device):
        return pltpu.make_async_remote_copy(
            src_ref=src, dst_ref=dst, send_sem=send_sem, recv_sem=recv_sem, device_id=device, device_id_type=MESH)

    def arrived(ref, sem):
        remote(ref, ref, hs_sem.at[0], sem, (o, sibling)).wait_recv()

    def sent(ref, sem):
        remote(ref, ref, sem, hr_sem.at[0], (o, sibling)).wait_send()

    for k in range(hist):
        with scope("hload"):
            if k == 0:
                landed(proj_ref, h_sem.at[hist])
            landed(hv.at[k], h_sem.at[k])
        with scope("project"):
            qh[s, k] = jnp.concatenate([
                lax.dot_general(hv[k, c], pv[c, cols(c, rank)], NT, preferred_element_type=F32)
                for c in range(clusters)], axis=1).astype(BF16)
        if k == 0:
            with scope("barrier"):
                pl.semaphore_wait(barrier, n_src + n_obs - 2)
        for pair in others:
            remote(qh.at[s, k], qh.at[s, k], hs_sem.at[0], hr_sem.at[k], (o, pair * 2 + mine)).start()
        remote(qh.at[s, k], qh.at[s, k], hs_sem.at[0], hf_sem.at[k], (o, sibling)).start()
        if k == 0:
            stack_loads(0, 0)
            near_load(0, 0)
    for j in range(1, tiles):
        near_load(0, j)
    for c in range(clusters):
        for k in range(clusters):
            if k != c:
                pv[c, cols(k, rank)] = jnp.zeros((rank, unknowns), BF16)
                xn[c, cols(k, rank)] = jnp.zeros((rank, unknowns), BF16)

    with scope("cload"):
        landed(lag_ref, l_sem.at[0])
        landed(coup_ref, c_sem.at[0])
    for c in range(1, clusters):
        stack_loads(c, 0)
        for j in range(tiles):
            near_load(c, j)
    for c in range(clusters):
        stack_loads(c, 1)
    lane = lax.broadcasted_iota(jnp.int32, (rank, width), 1)

    def build(j, carry):
        for p in range(2):
            cf[p] = cv[p, pl.ds(pl.multiple_of(j * (rank * n_obs), rank * n_obs), rank * n_obs), :].astype(F32)
        at = pl.ds(pl.multiple_of(j * rank, rank), rank)
        for to in range(n_obs):
            lag = jnp.full((rank, width), lag_ref[to, 0, j], jnp.int32)
            for k in range(1, clusters):
                lag = jnp.where(lane >= k * rank, lag_ref[to, k, j], lag)
            first = cf[0, pl.ds(to, rank, stride=n_obs), :]
            second = cf[1, pl.ds(to, rank, stride=n_obs), :]
            zero = jnp.zeros_like(first)
            one, two = lag == 1, lag == 2
            wv[0, at, cols(to, width)] = jnp.where(one, first, zero).astype(BF16)
            wv[1, at, cols(to, width)] = jnp.where(two, first, jnp.where(one, second, zero)).astype(BF16)
            wv[2, at, cols(to, width)] = jnp.where(two, second, zero).astype(BF16)
        return carry

    with scope("build"):
        lax.fori_loop(0, sources, build, 0)

    def near_tile(c, j, part):
        at = cols(j, tile)
        if part == 0:
            if j == 0:
                landed(av.at[c, :early], a_sem.at[c, 0])
            landed(nv.at[c, :, at], n_sem.at[c, j])
            value = jnp.dot(av[c, :early], nv[c, :, at], preferred_element_type=F32)
            yv[c, :early, at] = value
            xn[c, cols(c, rank), at] = value[soon * excite:].astype(BF16)
        else:
            if j == 0:
                landed(av.at[c, early:], a_sem.at[c, 1])
            yv[c, early:, at] = jnp.dot(av[c, early:], nv[c, :, at], preferred_element_type=F32)

    def near_end(c, part):
        which = slice(early) if part == 0 else slice(early, (steps + 1) * excite)
        value = lax.dot_general(yv[c, which].astype(BF16), pv[c], NT, preferred_element_type=F32)
        keep = slice(soon * excite) if part == 0 else slice(soon * excite, steps * excite)
        made = value[:soon * excite] if part == 0 else value
        if c == 0:
            bv[keep] = made
        else:
            bv[keep] += made
        if part == 0:
            mv[cols(c, rank)] = value[soon * excite:].astype(BF16)

    def near(c, part, chosen):
        for j in chosen:
            with scope(f"near{c}_{part}_{j}"):
                near_tile(c, j, part)
        if tiles - 1 in chosen:
            with scope(f"nearend{c}_{part}"):
                near_end(c, part)

    def rows_of(pair):
        return pl.ds(pl.multiple_of(pair * deep, deep), deep)

    def both(get, pair):
        return jnp.concatenate([get(pair * 2 + core) for core in range(2)], axis=1)

    def send_partial(step, total):
        for to in range(n_obs):
            sendp[step * n_obs + to] = total[:, cols(to, width)].astype(BF16)
        for peer in p_peers:
            remote(sendp.at[step * n_obs + peer], recvp.at[step * n_obs + o], ps_sem.at[0], pr_sem.at[step % 2],
                   (peer, s)).start()

    def slot_of(k):
        return jnp.concatenate([qh[j, k] for j in range(n_src)], axis=1)

    def forward(k):
        with scope("forward"):
            arrived(qh.at[pl.ds(0, pairs - 1), k], hr_sem.at[k])
            for pair in arriving:
                slot = pair * 2 + mine
                remote(qh.at[slot, k], qh.at[slot, k], hs_sem.at[0], hf_sem.at[k], (o, sibling)).start()

    for j in range(tiles):
        near(0, 0, range(j, j + 1))
        if 0 <= j + hist - 1 - tiles < hist - 1:
            forward(j + hist - 1 - tiles)
    forward(hist - 1)
    total = None
    for k in range(hist):
        with scope("hwait"):
            arrived(qh.at[pl.ds(0, pairs), k], hf_sem.at[k])
        with scope("first"):
            term = jnp.dot(slot_of(k), wv[hist - 1 - k], preferred_element_type=F32)
            total = term if total is None else total + term
    with scope("sendp"):
        send_partial(0, total)

    for c in range(1, clusters):
        near(c, 0, range(tiles))

    with scope("hbase"):
        for ahead in range(1, hist):
            total = None
            for d in range(ahead + 1, hist + 1):
                term = jnp.dot(slot_of(hist + ahead - d), wv[d - 1], preferred_element_type=F32)
                total = term if total is None else total + term
            base[ahead] = total
        for ahead in range(hist, steps):
            base[ahead] = jnp.zeros((excite, n_obs * width), F32)

    pending = [(c, 1, range(j, j + 1)) for c in range(clusters) for j in range(tiles)]
    shares = max(1, 2 * (soon - 1) + 2)
    share = -(-len(pending) // shares)

    def later(window):
        for c, part, chosen in pending[window * share:(window + 1) * share]:
            near(c, part, chosen)

    def newest_term(step, total):
        for place, pair in enumerate([own] + arriving):
            with scope(f"waitq{step}"):
                ready = qn.at[pl.ds(step * n_src + pair * 2, 2)] if place else qn.at[step * n_src + sibling]
                arrived(ready, qr_sem.at[step % 2, pair])
            part = both(lambda slot: qn[step * n_src + slot], pair)
            total = total + jnp.dot(part, wv[0, rows_of(pair), :], preferred_element_type=F32)
        return total

    def finish(step, field):
        for c in range(clusters):
            far = jnp.dot(field, xn[c], preferred_element_type=F32)
            out_ref[step, c] = (yv[c, cols(place(step), excite)] - far).astype(BF16)

    for step in range(steps):
        field = sendp[step * n_obs + o].astype(F32)
        with scope(f"waitp{step}"):
            arrived(recvp.at[pl.ds(0, n_obs - 1)], pr_sem.at[step % 2])
        for peer in p_peers:
            field = field + recvp[step * n_obs + peer].astype(F32)
        field = field.astype(BF16)
        if step + 1 == steps:
            with scope(f"finish{step}"):
                finish(step, field)
            break
        newest = bv[cols(step, excite)] - jnp.dot(field, mv[...], preferred_element_type=F32)
        qn[step * n_src + s] = newest.astype(BF16)
        for peer in q_peers:
            remote(qn.at[step * n_src + s], qn.at[step * n_src + s], qs_sem.at[0], qr_sem.at[step % 2, own],
                   (o, peer)).start()
        with scope(f"finish{step}"):
            finish(step, field)
        later(2 * step)
        with scope(f"newest{step}"):
            total = newest_term(step, base[step + 1])
        send_partial(step + 1, total)
        with scope(f"base{step}"):
            columns = jnp.concatenate([qn[step * n_src + j] for j in range(n_src)], axis=1)
            for d in range(2, hist + 1):
                if step + d < steps:
                    base[step + d] += jnp.dot(columns, wv[d - 1], preferred_element_type=F32)
        later(2 * step + 1)

    with scope("sent"):
        sent(qh.at[pl.ds(0, n_src - 1)], hs_sem.at[0])
        sent(qn.at[pl.ds(0, (steps - 1) * (n_src - 1))], qs_sem.at[0])
        sent(sendp.at[pl.ds(0, steps * (n_obs - 1))], ps_sem.at[0])


def hand_on(made_ref, out_ref, sem):
    for t in range(made_ref.shape[0]):
        pltpu.make_async_copy(made_ref.at[t], out_ref.at[t], sem.at[0]).start()
    pltpu.make_async_copy(made_ref, out_ref, sem.at[0]).wait()


def per_device(n_obs, n_src, history, incident, proj_basis, expand_basis, near_inverse, couplings, lags):
    hist, clusters, excite, unknowns = history.shape
    steps = incident.shape[0]
    rank = proj_basis.shape[1]
    width = clusters * rank
    taps, src_rows = couplings.shape[:2]
    sources = lags.shape[0]
    obs_cols = n_obs * width
    pairs = n_src // 2
    flat = couplings.reshape(taps, src_rows * n_obs, width)
    lag_table = jnp.transpose(lags.reshape(sources, n_obs, clusters), (1, 2, 0))
    stacked = (steps + 1) * excite
    any_spec = pl.BlockSpec(memory_space=pl.ANY)
    vmem_spec = pl.BlockSpec(memory_space=pltpu.VMEM)
    dma = pltpu.SemaphoreType.DMA
    made = pl.pallas_call(
        functools.partial(kernel, n_obs, n_src),
        out_shape=pltpu.VMEM(incident.shape, BF16),
        in_specs=[any_spec] * 7,
        out_specs=vmem_spec,
        scratch_shapes=[
            pltpu.SMEM((n_obs, clusters, sources), jnp.int32),
            pltpu.VMEM((hist, clusters, excite, unknowns), BF16),
            pltpu.VMEM((clusters, stacked, unknowns), BF16),
            pltpu.VMEM((clusters, width, unknowns), BF16),
            pltpu.VMEM((clusters, unknowns, unknowns), BF16),
            pltpu.VMEM((taps, src_rows * n_obs, width), BF16),
            pltpu.VMEM((taps, rank * n_obs, width), F32),
            pltpu.VMEM((hist, src_rows, obs_cols), BF16),
            pltpu.VMEM((clusters, stacked, unknowns), F32),
            pltpu.VMEM((clusters, width, unknowns), BF16),
            pltpu.VMEM((steps * excite, width), F32),
            pltpu.VMEM((width, width), BF16),
            pltpu.VMEM((n_src, hist, excite, width), BF16),
            pltpu.VMEM(((steps - 1) * n_src, excite, width), BF16),
            pltpu.VMEM((steps * n_obs, excite, width), BF16),
            pltpu.VMEM((steps * n_obs, excite, width), BF16),
            pltpu.VMEM((steps, excite, obs_cols), F32),
            dma((1,)),
            dma((hist + 1,)),
            dma((clusters, 2)),
            dma((1,)),
            dma((clusters, unknowns // 512)),
            dma((1,)),
            dma((hist,)),
            dma((hist,)),
            dma((1,)),
            dma((2, pairs)),
            dma((1,)),
            dma((2,)),
        ],
        compiler_params=pltpu.CompilerParams(
            collective_id=0, has_side_effects=True, vmem_limit_bytes=VMEM_LIMIT
        ),
    )(history, incident, proj_basis, expand_basis, near_inverse, flat, lag_table)
    return pl.pallas_call(
        hand_on,
        out_shape=jax.ShapeDtypeStruct(incident.shape, BF16),
        in_specs=[vmem_spec],
        out_specs=any_spec,
        scratch_shapes=[dma((1,))],
        compiler_params=pltpu.CompilerParams(vmem_limit_bytes=8000 * 1024),
    )(made)


def solution(mesh):
    placed = (
        P(None, ("obs", "src"), None, None),
        P(None, ("obs", "src"), None, None),
        P(("obs", "src"), None, None),
        P(("obs", "src"), None, None),
        P(("obs", "src"), None, None),
        P(None, "obs", None, "src", None),
        P("obs", None, "src", None),
    )
    return jax.shard_map(
        functools.partial(per_device, mesh.shape["obs"], mesh.shape["src"]),
        mesh=mesh,
        in_specs=placed,
        out_specs=P(None, ("obs", "src"), None, None),
        check_vma=False,
    )
```

```python
import contextlib
import functools

import jax
import jax.numpy as jnp
from jax import lax
from jax.experimental import pallas as pl
from jax.experimental.pallas import tpu as pltpu
from jax.sharding import PartitionSpec as P

MESH = pl.DeviceIdType.MESH
F32 = jnp.float32
BF16 = jnp.bfloat16
NT = (((1,), (1,)), ((), ()))
VMEM_LIMIT = 60000 * 1024


def scope(name):
    return contextlib.nullcontext()


def flipped(me, bits, count):
    other = me
    place = 1
    while place < count:
        if bits & place:
            other = other + (1 - 2 * ((me // place) % 2)) * place
        place *= 2
    return other


def partner(me, turn, count):
    if count & (count - 1) == 0:
        return flipped(me, count - turn, count)
    return lax.rem(me + turn, count)


def farthest_first(me, count):
    upper = (2 * me) // count
    sign = 1 - 2 * upper
    near_end = me * (1 - upper) + (count - 1 - me) * upper
    peers = []
    for i in range(count - 1):
        one_sided = (3 * count - 2 - i - 2 * near_end) // (2 * count)
        left = count - 2 - i
        paired = (left // 2 + 1) * (2 * (left % 2) - 1)
        peers.append(me + sign * (one_sided * (count - 1 - near_end - i) + (1 - one_sided) * paired))
    return peers


def kernel(n_obs, n_src, hist_ref, inc_ref, proj_ref, expand_ref, near_ref, coup_ref, lags_ref, out_ref,
           lag_ref, hv, av, pv, nv, cv, cf, wv, yv, xn, bv, mv, qh, qn, sendp, recvp, base,
           l_sem, h_sem, a_sem, c_sem, n_sem, hs_sem, hr_sem, hf_sem, qs_sem, qr_sem, ps_sem, pr_sem):
    o = lax.axis_index("obs")
    s = lax.axis_index("src")
    hist, clusters, excite, unknowns = hist_ref.shape
    steps = inc_ref.shape[0]
    rank = proj_ref.shape[1]
    width = clusters * rank
    sources = lag_ref.shape[2]
    tile = 512
    tiles = unknowns // tile
    pairs = n_src // 2
    deep = 2 * width

    soon = min(2, steps)
    early = (soon + 1) * excite

    def place(step):
        return step if step < soon else step + 1

    def rows(index, size):
        return pl.ds(index * size, size)

    def cols(index, size):
        return slice(index * size, (index + 1) * size)

    def local(src, dst, sem):
        pltpu.make_async_copy(src, dst, sem).start()

    def landed(ref, sem):
        pltpu.make_async_copy(ref, ref, sem).wait()

    for c in range(clusters):
        local(proj_ref.at[c], pv.at[c, rows(c, rank)], h_sem.at[hist])
    for k in range(hist):
        for c in range(clusters):
            local(hist_ref.at[k, c], hv.at[k, c], h_sem.at[k])

    mine = s % 2
    own = s // 2
    sibling = s + 1 - 2 * mine
    others = [partner(own, turn, pairs) for turn in range(1, pairs)]
    arriving = [partner(own, turn, pairs) for turn in range(pairs - 1, 0, -1)]
    q_peers = [pair * 2 + core for pair in others for core in range(2)] + [sibling]
    p_peers = farthest_first(o, n_obs)

    barrier = pltpu.get_barrier_semaphore()
    for peer in q_peers:
        pl.semaphore_signal(barrier, inc=1, device_id=(o, peer), device_id_type=MESH)
    for peer in p_peers:
        pl.semaphore_signal(barrier, inc=1, device_id=(peer, s), device_id_type=MESH)

    local(lags_ref, lag_ref, l_sem.at[0])
    quarter = coup_ref.shape[1] // 4
    for p in range(coup_ref.shape[0]):
        for part in range(4):
            local(coup_ref.at[p, rows(part, quarter)], cv.at[p, rows(part, quarter)], c_sem.at[0])


    def stack_loads(c, part):
        for t in range(soon) if part == 0 else range(soon, steps):
            local(inc_ref.at[t, c], av.at[c, rows(place(t), excite)], a_sem.at[c, part])
        if part == 0:
            local(expand_ref.at[c], av.at[c, rows(soon, excite)], a_sem.at[c, part])

    def near_load(c, j):
        local(near_ref.at[c, :, cols(j, tile)], nv.at[c, :, cols(j, tile)], n_sem.at[c, j])


    def remote(src, dst, send_sem, recv_sem, device):
        return pltpu.make_async_remote_copy(
            src_ref=src, dst_ref=dst, send_sem=send_sem, recv_sem=recv_sem, device_id=device, device_id_type=MESH)

    def arrived(ref, sem):
        remote(ref, ref, hs_sem.at[0], sem, (o, sibling)).wait_recv()

    def sent(ref, sem):
        remote(ref, ref, sem, hr_sem.at[0], (o, sibling)).wait_send()

    for k in range(hist):
        with scope("hload"):
            if k == 0:
                landed(proj_ref, h_sem.at[hist])
            landed(hv.at[k], h_sem.at[k])
        with scope("project"):
            qh[s, k] = jnp.concatenate([
                lax.dot_general(hv[k, c], pv[c, cols(c, rank)], NT, preferred_element_type=F32)
                for c in range(clusters)], axis=1).astype(BF16)
        if k == 0:
            with scope("barrier"):
                pl.semaphore_wait(barrier, n_src + n_obs - 2)
        for pair in others:
            remote(qh.at[s, k], qh.at[s, k], hs_sem.at[0], hr_sem.at[k], (o, pair * 2 + mine)).start()
        remote(qh.at[s, k], qh.at[s, k], hs_sem.at[0], hf_sem.at[k], (o, sibling)).start()
        if k == 0:
            stack_loads(0, 0)
            near_load(0, 0)
    for j in range(1, tiles):
        near_load(0, j)
    for c in range(clusters):
        for k in range(clusters):
            if k != c:
                pv[c, cols(k, rank)] = jnp.zeros((rank, unknowns), BF16)
                xn[c, cols(k, rank)] = jnp.zeros((rank, unknowns), BF16)

    with scope("cload"):
        landed(lag_ref, l_sem.at[0])
        landed(coup_ref, c_sem.at[0])
    for c in range(1, clusters):
        stack_loads(c, 0)
        for j in range(tiles):
            near_load(c, j)
    for c in range(clusters):
        stack_loads(c, 1)
    lane = lax.broadcasted_iota(jnp.int32, (rank, width), 1)

    def build(j, carry):
        for p in range(2):
            cf[p] = cv[p, pl.ds(pl.multiple_of(j * (rank * n_obs), rank * n_obs), rank * n_obs), :].astype(F32)
        at = pl.ds(pl.multiple_of(j * rank, rank), rank)
        for to in range(n_obs):
            lag = jnp.full((rank, width), lag_ref[to, 0, j], jnp.int32)
            for k in range(1, clusters):
                lag = jnp.where(lane >= k * rank, lag_ref[to, k, j], lag)
            first = cf[0, pl.ds(to, rank, stride=n_obs), :]
            second = cf[1, pl.ds(to, rank, stride=n_obs), :]
            zero = jnp.zeros_like(first)
            one, two = lag == 1, lag == 2
            wv[0, at, cols(to, width)] = jnp.where(one, first, zero).astype(BF16)
            wv[1, at, cols(to, width)] = jnp.where(two, first, jnp.where(one, second, zero)).astype(BF16)
            wv[2, at, cols(to, width)] = jnp.where(two, second, zero).astype(BF16)
        return carry

    with scope("build"):
        lax.fori_loop(0, sources, build, 0)

    def near_tile(c, j, part):
        at = cols(j, tile)
        if part == 0:
            if j == 0:
                landed(av.at[c, :early], a_sem.at[c, 0])
            landed(nv.at[c, :, at], n_sem.at[c, j])
            value = jnp.dot(av[c, :early], nv[c, :, at], preferred_element_type=F32)
            yv[c, :early, at] = value
            xn[c, cols(c, rank), at] = value[soon * excite:].astype(BF16)
        else:
            if j == 0:
                landed(av.at[c, early:], a_sem.at[c, 1])
            yv[c, early:, at] = jnp.dot(av[c, early:], nv[c, :, at], preferred_element_type=F32)

    def near_end(c, part):
        which = slice(early) if part == 0 else slice(early, (steps + 1) * excite)
        value = lax.dot_general(yv[c, which].astype(BF16), pv[c], NT, preferred_element_type=F32)
        keep = slice(soon * excite) if part == 0 else slice(soon * excite, steps * excite)
        made = value[:soon * excite] if part == 0 else value
        if c == 0:
            bv[keep] = made
        else:
            bv[keep] += made
        if part == 0:
            mv[cols(c, rank)] = value[soon * excite:].astype(BF16)

    def near(c, part, chosen):
        for j in chosen:
            with scope(f"near{c}_{part}_{j}"):
                near_tile(c, j, part)
        if tiles - 1 in chosen:
            with scope(f"nearend{c}_{part}"):
                near_end(c, part)

    def rows_of(pair):
        return pl.ds(pl.multiple_of(pair * deep, deep), deep)

    def both(get, pair):
        return jnp.concatenate([get(pair * 2 + core) for core in range(2)], axis=1)

    def send_partial(step, total):
        for to in range(n_obs):
            sendp[step * n_obs + to] = total[:, cols(to, width)].astype(BF16)
        for peer in p_peers:
            remote(sendp.at[step * n_obs + peer], recvp.at[step * n_obs + o], ps_sem.at[0], pr_sem.at[step % 2],
                   (peer, s)).start()

    def slot_of(k):
        return jnp.concatenate([qh[j, k] for j in range(n_src)], axis=1)

    def forward(k):
        with scope("forward"):
            arrived(qh.at[pl.ds(0, pairs - 1), k], hr_sem.at[k])
            for pair in arriving:
                slot = pair * 2 + mine
                remote(qh.at[slot, k], qh.at[slot, k], hs_sem.at[0], hf_sem.at[k], (o, sibling)).start()

    def first(k):
        with scope("hwait"):
            arrived(qh.at[pl.ds(0, pairs), k], hf_sem.at[k])
        with scope("first"):
            term = jnp.dot(slot_of(k), wv[hist - 1 - k], preferred_element_type=F32)
            base[0] = term if k == 0 else base[0] + term

    for j in range(tiles):
        with scope(f"near0_0_{j}"):
            near_tile(0, j, 0)
    for k in range(hist):
        forward(k)
    for k in range(hist - 1):
        first(k)
    with scope("hwait"):
        arrived(qh.at[pl.ds(0, pairs), hist - 1], hf_sem.at[hist - 1])
    with scope("sendp"):
        term = jnp.dot(slot_of(hist - 1), wv[0], preferred_element_type=F32)
        send_partial(0, base[0] + term)

    with scope("nearend0_0"):
        near_end(0, 0)
    for c in range(1, clusters):
        near(c, 0, range(tiles))

    pending = [(c, 1, range(j, j + 1)) for c in range(clusters) for j in range(tiles)]
    shares = max(1, 2 * (soon - 1) + 2)
    share = -(-len(pending) // shares)

    def later(window):
        for c, part, chosen in pending[window * share:(window + 1) * share]:
            near(c, part, chosen)

    def newest_term(step):
        total = base[step + 1]
        for place, pair in enumerate([own] + arriving):
            with scope(f"waitq{step}"):
                ready = qn.at[pl.ds(step * n_src + pair * 2, 2)] if place else qn.at[step * n_src + sibling]
                arrived(ready, qr_sem.at[step % 2, pair])
            part = both(lambda slot: qn[step * n_src + slot], pair)
            total = total + jnp.dot(part, wv[0, rows_of(pair), :], preferred_element_type=F32)
        return total

    def older_terms():
        with scope("hbase"):
            for ahead in range(1, hist):
                total = None
                for d in range(ahead + 1, hist + 1):
                    term = jnp.dot(slot_of(hist + ahead - d), wv[d - 1], preferred_element_type=F32)
                    total = term if total is None else total + term
                base[ahead] = total
            for ahead in range(hist, steps):
                base[ahead] = jnp.zeros((excite, n_obs * width), F32)

    def finish(step, field):
        for c in range(clusters):
            far = jnp.dot(field, xn[c], preferred_element_type=F32)
            out_ref[step, c] = (yv[c, cols(place(step), excite)] - far).astype(BF16)

    for step in range(steps):
        field = sendp[step * n_obs + o].astype(F32)
        with scope(f"waitp{step}"):
            arrived(recvp.at[pl.ds(0, n_obs - 1)], pr_sem.at[step % 2])
        for peer in p_peers:
            field = field + recvp[step * n_obs + peer].astype(F32)
        field = field.astype(BF16)
        if step + 1 == steps:
            with scope(f"finish{step}"):
                finish(step, field)
            break
        newest = bv[cols(step, excite)] - jnp.dot(field, mv[...], preferred_element_type=F32)
        qn[step * n_src + s] = newest.astype(BF16)
        for peer in q_peers:
            remote(qn.at[step * n_src + s], qn.at[step * n_src + s], qs_sem.at[0], qr_sem.at[step % 2, own],
                   (o, peer)).start()
        with scope(f"finish{step}"):
            finish(step, field)
        if step == 0:
            older_terms()
        later(2 * step)
        with scope(f"newest{step}"):
            total = newest_term(step)
        send_partial(step + 1, total)
        with scope(f"base{step}"):
            columns = jnp.concatenate([qn[step * n_src + j] for j in range(n_src)], axis=1)
            for d in range(2, hist + 1):
                if step + d < steps:
                    base[step + d] += jnp.dot(columns, wv[d - 1], preferred_element_type=F32)
        later(2 * step + 1)

    with scope("sent"):
        sent(qh.at[pl.ds(0, n_src - 1)], hs_sem.at[0])
        sent(qn.at[pl.ds(0, (steps - 1) * (n_src - 1))], qs_sem.at[0])
        sent(sendp.at[pl.ds(0, steps * (n_obs - 1))], ps_sem.at[0])


def hand_on(made_ref, out_ref, sem):
    for t in range(made_ref.shape[0]):
        pltpu.make_async_copy(made_ref.at[t], out_ref.at[t], sem.at[0]).start()
    pltpu.make_async_copy(made_ref, out_ref, sem.at[0]).wait()


def per_device(n_obs, n_src, history, incident, proj_basis, expand_basis, near_inverse, couplings, lags):
    hist, clusters, excite, unknowns = history.shape
    steps = incident.shape[0]
    rank = proj_basis.shape[1]
    width = clusters * rank
    taps, src_rows = couplings.shape[:2]
    sources = lags.shape[0]
    obs_cols = n_obs * width
    pairs = n_src // 2
    flat = couplings.reshape(taps, src_rows * n_obs, width)
    lag_table = jnp.transpose(lags.reshape(sources, n_obs, clusters), (1, 2, 0))
    stacked = (steps + 1) * excite
    any_spec = pl.BlockSpec(memory_space=pl.ANY)
    vmem_spec = pl.BlockSpec(memory_space=pltpu.VMEM)
    dma = pltpu.SemaphoreType.DMA
    made = pl.pallas_call(
        functools.partial(kernel, n_obs, n_src),
        out_shape=pltpu.VMEM(incident.shape, BF16),
        in_specs=[any_spec] * 7,
        out_specs=vmem_spec,
        scratch_shapes=[
            pltpu.SMEM((n_obs, clusters, sources), jnp.int32),
            pltpu.VMEM((hist, clusters, excite, unknowns), BF16),
            pltpu.VMEM((clusters, stacked, unknowns), BF16),
            pltpu.VMEM((clusters, width, unknowns), BF16),
            pltpu.VMEM((clusters, unknowns, unknowns), BF16),
            pltpu.VMEM((taps, src_rows * n_obs, width), BF16),
            pltpu.VMEM((taps, rank * n_obs, width), F32),
            pltpu.VMEM((hist, src_rows, obs_cols), BF16),
            pltpu.VMEM((clusters, stacked, unknowns), F32),
            pltpu.VMEM((clusters, width, unknowns), BF16),
            pltpu.VMEM((steps * excite, width), F32),
            pltpu.VMEM((width, width), BF16),
            pltpu.VMEM((n_src, hist, excite, width), BF16),
            pltpu.VMEM(((steps - 1) * n_src, excite, width), BF16),
            pltpu.VMEM((steps * n_obs, excite, width), BF16),
            pltpu.VMEM((steps * n_obs, excite, width), BF16),
            pltpu.VMEM((steps, excite, obs_cols), F32),
            dma((1,)),
            dma((hist + 1,)),
            dma((clusters, 2)),
            dma((1,)),
            dma((clusters, unknowns // 512)),
            dma((1,)),
            dma((hist,)),
            dma((hist,)),
            dma((1,)),
            dma((2, pairs)),
            dma((1,)),
            dma((2,)),
        ],
        compiler_params=pltpu.CompilerParams(
            collective_id=0, has_side_effects=True, vmem_limit_bytes=VMEM_LIMIT
        ),
    )(history, incident, proj_basis, expand_basis, near_inverse, flat, lag_table)
    return pl.pallas_call(
        hand_on,
        out_shape=jax.ShapeDtypeStruct(incident.shape, BF16),
        in_specs=[vmem_spec],
        out_specs=any_spec,
        scratch_shapes=[dma((1,))],
        compiler_params=pltpu.CompilerParams(vmem_limit_bytes=8000 * 1024),
    )(made)


def solution(mesh):
    placed = (
        P(None, ("obs", "src"), None, None),
        P(None, ("obs", "src"), None, None),
        P(("obs", "src"), None, None),
        P(("obs", "src"), None, None),
        P(("obs", "src"), None, None),
        P(None, "obs", None, "src", None),
        P("obs", None, "src", None),
    )
    return jax.shard_map(
        functools.partial(per_device, mesh.shape["obs"], mesh.shape["src"]),
        mesh=mesh,
        in_specs=placed,
        out_specs=P(None, ("obs", "src"), None, None),
        check_vma=False,
    )
```

```python
import contextlib
import functools

import jax
import jax.numpy as jnp
from jax import lax
from jax.experimental import pallas as pl
from jax.experimental.pallas import tpu as pltpu
from jax.sharding import PartitionSpec as P

MESH = pl.DeviceIdType.MESH
F32 = jnp.float32
BF16 = jnp.bfloat16
NT = (((1,), (1,)), ((), ()))
VMEM_LIMIT = 60000 * 1024


def scope(name):
    return contextlib.nullcontext()


def flipped(me, bits, count):
    other = me
    place = 1
    while place < count:
        if bits & place:
            other = other + (1 - 2 * ((me // place) % 2)) * place
        place *= 2
    return other


def partner(me, turn, count):
    if count & (count - 1) == 0:
        return flipped(me, count - turn, count)
    return lax.rem(me + turn, count)


def sender(me, turn, count):
    if count & (count - 1) == 0:
        return partner(me, turn, count)
    return lax.rem(me + count - turn, count)


def farthest_first(me, count):
    upper = (2 * me) // count
    sign = 1 - 2 * upper
    near_end = me * (1 - upper) + (count - 1 - me) * upper
    peers = []
    for i in range(count - 1):
        one_sided = (3 * count - 2 - i - 2 * near_end) // (2 * count)
        left = count - 2 - i
        paired = (left // 2 + 1) * (2 * (left % 2) - 1)
        peers.append(me + sign * (one_sided * (count - 1 - near_end - i) + (1 - one_sided) * paired))
    return peers


def kernel(n_obs, n_src, hist_ref, inc_ref, proj_ref, expand_ref, near_ref, coup_ref, lags_ref, out_ref,
           lag_ref, hv, av, pv, nv, cv, cf, wv, yv, xn, bv, mv, qh, qn, sendp, recvp, base,
           l_sem, hs_sem, hr_sem, hf_sem, qr_sem, ps_sem, pr_sem):
    o = lax.axis_index("obs")
    s = lax.axis_index("src")
    hist, clusters, excite, unknowns = hist_ref.shape
    steps = inc_ref.shape[0]
    rank = proj_ref.shape[1]
    width = clusters * rank
    sources = lag_ref.shape[2]
    tile = 512
    tiles = unknowns // tile
    pairs = n_src // 2
    deep = 2 * width

    soon = min(2, steps)
    early = (soon + 1) * excite

    def place(step):
        return step if step < soon else step + 1

    def rows(index, size):
        return pl.ds(index * size, size)

    def cols(index, size):
        return slice(index * size, (index + 1) * size)

    def local(src, dst, sem):
        pltpu.make_async_copy(src, dst, sem).start()

    def landed(ref, sem):
        pltpu.make_async_copy(ref, ref, sem).wait()

    for c in range(clusters):
        local(proj_ref.at[c], pv.at[c, rows(c, rank)], l_sem.at[0])
    for k in range(hist):
        for c in range(clusters):
            local(hist_ref.at[k, c], hv.at[k, c], l_sem.at[1 + k])

    mine = s % 2
    own = s // 2
    sibling = s + 1 - 2 * mine
    others = [partner(own, turn, pairs) for turn in range(1, pairs)]
    arriving = [sender(own, turn, pairs) for turn in range(pairs - 1, 0, -1)]
    q_peers = [pair * 2 + core for pair in others for core in range(2)] + [sibling]
    p_peers = farthest_first(o, n_obs)

    barrier = pltpu.get_barrier_semaphore()
    for peer in q_peers:
        pl.semaphore_signal(barrier, inc=1, device_id=(o, peer), device_id_type=MESH)
    for peer in p_peers:
        pl.semaphore_signal(barrier, inc=1, device_id=(peer, s), device_id_type=MESH)

    local(lags_ref, lag_ref, l_sem.at[hist + 1])
    quarter = coup_ref.shape[1] // 4
    for p in range(coup_ref.shape[0]):
        for part in range(4):
            local(coup_ref.at[p, rows(part, quarter)], cv.at[p, rows(part, quarter)], l_sem.at[hist + 2])


    def stack_sem(c):
        return l_sem.at[0] if c == 0 else l_sem.at[hist - 1 + 2 * c]

    def near_sem(c, j):
        return l_sem.at[1 + j] if c == 0 else l_sem.at[hist + 2 * c]

    late_sem = l_sem.at[hist + 1 + 2 * max(1, clusters - 1)]

    def stack_loads(c, part):
        for t in range(soon) if part == 0 else range(soon, steps):
            local(inc_ref.at[t, c], av.at[c, rows(place(t), excite)], stack_sem(c) if part == 0 else late_sem)
        if part == 0:
            local(expand_ref.at[c], av.at[c, rows(soon, excite)], stack_sem(c))

    def near_load(c, j):
        local(near_ref.at[c, :, cols(j, tile)], nv.at[c, :, cols(j, tile)], near_sem(c, j))

    def remote(src, dst, send_sem, recv_sem, device):
        return pltpu.make_async_remote_copy(
            src_ref=src, dst_ref=dst, send_sem=send_sem, recv_sem=recv_sem, device_id=device, device_id_type=MESH)

    def arrived(ref, sem):
        remote(ref, ref, hs_sem.at[0], sem, (o, sibling)).wait_recv()

    def sent(ref, sem):
        remote(ref, ref, sem, hr_sem.at[0], (o, sibling)).wait_send()

    for k in range(hist):
        with scope("hload"):
            if k == 0:
                landed(proj_ref, l_sem.at[0])
            landed(hv.at[k], l_sem.at[1 + k])
        with scope("project"):
            qh[s, k] = jnp.concatenate([
                lax.dot_general(hv[k, c], pv[c, cols(c, rank)], NT, preferred_element_type=F32)
                for c in range(clusters)], axis=1).astype(BF16)
        if k == 0:
            with scope("barrier"):
                pl.semaphore_wait(barrier, n_src + n_obs - 2)
        for pair in others:
            remote(qh.at[s, k], qh.at[s, k], hs_sem.at[0], hr_sem.at[k], (o, pair * 2 + mine)).start()
        remote(qh.at[s, k], qh.at[s, k], hs_sem.at[0], hf_sem.at[k], (o, sibling)).start()
        if k == 0:
            stack_loads(0, 0)
            near_load(0, 0)
    for j in range(1, tiles):
        near_load(0, j)
    for c in range(clusters):
        for k in range(clusters):
            if k != c:
                pv[c, cols(k, rank)] = jnp.zeros((rank, unknowns), BF16)
                xn[c, cols(k, rank)] = jnp.zeros((rank, unknowns), BF16)

    with scope("cload"):
        landed(lag_ref, l_sem.at[hist + 1])
        landed(coup_ref, l_sem.at[hist + 2])
    for c in range(1, clusters):
        stack_loads(c, 0)
        for j in range(tiles):
            near_load(c, j)
    for c in range(clusters):
        stack_loads(c, 1)
    lane = lax.broadcasted_iota(jnp.int32, (rank, width), 1)

    def build(j, carry):
        for p in range(2):
            cf[p] = cv[p, pl.ds(pl.multiple_of(j * (rank * n_obs), rank * n_obs), rank * n_obs), :].astype(F32)
        at = pl.ds(pl.multiple_of(j * rank, rank), rank)
        for to in range(n_obs):
            lag = jnp.full((rank, width), lag_ref[to, 0, j], jnp.int32)
            for k in range(1, clusters):
                lag = jnp.where(lane >= k * rank, lag_ref[to, k, j], lag)
            first = cf[0, pl.ds(to, rank, stride=n_obs), :]
            second = cf[1, pl.ds(to, rank, stride=n_obs), :]
            zero = jnp.zeros_like(first)
            one, two = lag == 1, lag == 2
            wv[0, at, cols(to, width)] = jnp.where(one, first, zero).astype(BF16)
            wv[1, at, cols(to, width)] = jnp.where(two, first, jnp.where(one, second, zero)).astype(BF16)
            wv[2, at, cols(to, width)] = jnp.where(two, second, zero).astype(BF16)
        return carry

    with scope("build"):
        lax.fori_loop(0, sources, build, 0)

    def near_tile(c, j, part):
        at = cols(j, tile)
        if part == 0:
            if j == 0:
                landed(av.at[c, :early], stack_sem(c))
            if c == 0:
                landed(nv.at[c, :, at], near_sem(c, j))
            elif j == 0:
                landed(nv.at[c], near_sem(c, j))
            value = jnp.dot(av[c, :early], nv[c, :, at], preferred_element_type=F32)
            yv[c, :early, at] = value
            xn[c, cols(c, rank), at] = value[soon * excite:].astype(BF16)
        else:
            if c == 0 and j == 0:
                landed(av.at[:, early:], late_sem)
            yv[c, early:, at] = jnp.dot(av[c, early:], nv[c, :, at], preferred_element_type=F32)

    def near_end(c, part):
        which = slice(early) if part == 0 else slice(early, (steps + 1) * excite)
        value = lax.dot_general(yv[c, which].astype(BF16), pv[c], NT, preferred_element_type=F32)
        keep = slice(soon * excite) if part == 0 else slice(soon * excite, steps * excite)
        made = value[:soon * excite] if part == 0 else value
        if c == 0:
            bv[keep] = made
        else:
            bv[keep] += made
        if part == 0:
            mv[cols(c, rank)] = value[soon * excite:].astype(BF16)

    def near(c, part, chosen):
        for j in chosen:
            with scope(f"near{c}_{part}_{j}"):
                near_tile(c, j, part)
        if tiles - 1 in chosen:
            with scope(f"nearend{c}_{part}"):
                near_end(c, part)

    def rows_of(pair):
        return pl.ds(pl.multiple_of(pair * deep, deep), deep)

    def both(get, pair):
        return jnp.concatenate([get(pair * 2 + core) for core in range(2)], axis=1)

    def p_sem(step):
        return hr_sem.at[0] if step % 2 else pr_sem.at[0]

    def q_sem(step, group):
        return hf_sem.at[group] if step % 2 else qr_sem.at[group]

    def send_partial(step, total):
        for to in range(n_obs):
            sendp[step * n_obs + to] = total[:, cols(to, width)].astype(BF16)
        for peer in p_peers:
            remote(sendp.at[step * n_obs + peer], recvp.at[step * n_obs + o], ps_sem.at[0], p_sem(step),
                   (peer, s)).start()

    def slot_of(k):
        return jnp.concatenate([qh[j, k] for j in range(n_src)], axis=1)

    def forward(k):
        with scope("forward"):
            arrived(qh.at[pl.ds(0, pairs - 1), k], hr_sem.at[k])
            for pair in arriving:
                slot = pair * 2 + mine
                remote(qh.at[slot, k], qh.at[slot, k], hs_sem.at[0], hf_sem.at[k], (o, sibling)).start()

    def first(k):
        with scope("hwait"):
            arrived(qh.at[pl.ds(0, pairs), k], hf_sem.at[k])
        with scope("first"):
            term = jnp.dot(slot_of(k), wv[hist - 1 - k], preferred_element_type=F32)
            base[0] = term if k == 0 else base[0] + term

    for j in range(tiles):
        with scope(f"near0_0_{j}"):
            near_tile(0, j, 0)
    for k in range(hist):
        forward(k)
    for k in range(hist - 1):
        first(k)
    with scope("hwait"):
        arrived(qh.at[pl.ds(0, pairs), hist - 1], hf_sem.at[hist - 1])
    with scope("sendp"):
        term = jnp.dot(slot_of(hist - 1), wv[0], preferred_element_type=F32)
        send_partial(0, base[0] + term)

    with scope("nearend0_0"):
        near_end(0, 0)
    for c in range(1, clusters):
        near(c, 0, range(tiles))

    sent(qh.at[pl.ds(0, n_src - 1)], hs_sem.at[0])
    pending = [(c, 1, range(j, j + 1)) for c in range(clusters) for j in range(tiles)]
    shares = max(1, 2 * (soon - 1) + 2)
    share = -(-len(pending) // shares)

    def later(window):
        for c, part, chosen in pending[window * share:(window + 1) * share]:
            near(c, part, chosen)

    def newest_term(step):
        total = base[step + 1]
        for turn, pair in enumerate([own] + arriving):
            with scope(f"waitq{step}"):
                if turn == 0:
                    arrived(qn.at[step * n_src + sibling], q_sem(step, 0))
                elif turn == 1 and pairs > 2:
                    arrived(qn.at[pl.ds(step * n_src, 2 * (pairs - 2))], q_sem(step, 1))
                elif turn == pairs - 1:
                    arrived(qn.at[pl.ds(step * n_src + pair * 2, 2)], q_sem(step, 2))
            part = both(lambda slot: qn[step * n_src + slot], pair)
            total = total + jnp.dot(part, wv[0, rows_of(pair), :], preferred_element_type=F32)
        return total

    def older_terms():
        with scope("hbase"):
            for ahead in range(1, hist):
                total = None
                for d in range(ahead + 1, hist + 1):
                    term = jnp.dot(slot_of(hist + ahead - d), wv[d - 1], preferred_element_type=F32)
                    total = term if total is None else total + term
                base[ahead] = total
            for ahead in range(hist, steps):
                base[ahead] = jnp.zeros((excite, n_obs * width), F32)

    def finish(step, field):
        for c in range(clusters):
            far = jnp.dot(field, xn[c], preferred_element_type=F32)
            out_ref[step, c] = (yv[c, cols(place(step), excite)] - far).astype(BF16)

    for step in range(steps):
        field = sendp[step * n_obs + o].astype(F32)
        with scope(f"waitp{step}"):
            arrived(recvp.at[pl.ds(0, n_obs - 1)], p_sem(step))
        for peer in p_peers:
            field = field + recvp[step * n_obs + peer].astype(F32)
        field = field.astype(BF16)
        if step + 1 == steps:
            with scope(f"finish{step}"):
                finish(step, field)
            break
        newest = bv[cols(step, excite)] - jnp.dot(field, mv[...], preferred_element_type=F32)
        qn[step * n_src + s] = newest.astype(BF16)
        for turn, peer in enumerate(q_peers):
            group = 2 if turn < 2 else 1 if peer is not sibling else 0
            remote(qn.at[step * n_src + s], qn.at[step * n_src + s], hs_sem.at[0], q_sem(step, group),
                   (o, peer)).start()
        with scope(f"finish{step}"):
            finish(step, field)
        if step == 0:
            older_terms()
        later(2 * step)
        with scope(f"newest{step}"):
            total = newest_term(step)
        send_partial(step + 1, total)
        with scope(f"base{step}"):
            columns = jnp.concatenate([qn[step * n_src + j] for j in range(n_src)], axis=1)
            for d in range(2, hist + 1):
                if step + d < steps:
                    base[step + d] += jnp.dot(columns, wv[d - 1], preferred_element_type=F32)
        later(2 * step + 1)

    with scope("sent"):
        sent(qn.at[pl.ds(0, (steps - 1) * (n_src - 1))], hs_sem.at[0])
        sent(sendp.at[pl.ds(0, steps * (n_obs - 1))], ps_sem.at[0])


def hand_on(made_ref, out_ref, sem):
    for t in range(made_ref.shape[0]):
        pltpu.make_async_copy(made_ref.at[t], out_ref.at[t], sem.at[0]).start()
    pltpu.make_async_copy(made_ref, out_ref, sem.at[0]).wait()


def per_device(n_obs, n_src, history, incident, proj_basis, expand_basis, near_inverse, couplings, lags):
    hist, clusters, excite, unknowns = history.shape
    steps = incident.shape[0]
    rank = proj_basis.shape[1]
    width = clusters * rank
    taps, src_rows = couplings.shape[:2]
    sources = lags.shape[0]
    obs_cols = n_obs * width
    pairs = n_src // 2
    flat = couplings.reshape(taps, src_rows * n_obs, width)
    lag_table = jnp.transpose(lags.reshape(sources, n_obs, clusters), (1, 2, 0))
    stacked = (steps + 1) * excite
    any_spec = pl.BlockSpec(memory_space=pl.ANY)
    vmem_spec = pl.BlockSpec(memory_space=pltpu.VMEM)
    dma = pltpu.SemaphoreType.DMA
    made = pl.pallas_call(
        functools.partial(kernel, n_obs, n_src),
        out_shape=pltpu.VMEM(incident.shape, BF16),
        in_specs=[any_spec] * 7,
        out_specs=vmem_spec,
        scratch_shapes=[
            pltpu.SMEM((n_obs, clusters, sources), jnp.int32),
            pltpu.VMEM((hist, clusters, excite, unknowns), BF16),
            pltpu.VMEM((clusters, stacked, unknowns), BF16),
            pltpu.VMEM((clusters, width, unknowns), BF16),
            pltpu.VMEM((clusters, unknowns, unknowns), BF16),
            pltpu.VMEM((taps, src_rows * n_obs, width), BF16),
            pltpu.VMEM((taps, rank * n_obs, width), F32),
            pltpu.VMEM((hist, src_rows, obs_cols), BF16),
            pltpu.VMEM((clusters, stacked, unknowns), F32),
            pltpu.VMEM((clusters, width, unknowns), BF16),
            pltpu.VMEM((steps * excite, width), F32),
            pltpu.VMEM((width, width), BF16),
            pltpu.VMEM((n_src, hist, excite, width), BF16),
            pltpu.VMEM(((steps - 1) * n_src, excite, width), BF16),
            pltpu.VMEM((steps * n_obs, excite, width), BF16),
            pltpu.VMEM((steps * n_obs, excite, width), BF16),
            pltpu.VMEM((steps, excite, obs_cols), F32),
            dma((hist + 2 + 2 * max(1, clusters - 1),)),
            dma((1,)),
            dma((hist,)),
            dma((max(hist, 3),)),
            dma((3,)),
            dma((1,)),
            dma((1,)),
        ],
        compiler_params=pltpu.CompilerParams(
            collective_id=0, has_side_effects=True, vmem_limit_bytes=VMEM_LIMIT
        ),
    )(history, incident, proj_basis, expand_basis, near_inverse, flat, lag_table)
    return pl.pallas_call(
        hand_on,
        out_shape=jax.ShapeDtypeStruct(incident.shape, BF16),
        in_specs=[vmem_spec],
        out_specs=any_spec,
        scratch_shapes=[dma((1,))],
        compiler_params=pltpu.CompilerParams(vmem_limit_bytes=8000 * 1024),
    )(made)


def solution(mesh):
    placed = (
        P(None, ("obs", "src"), None, None),
        P(None, ("obs", "src"), None, None),
        P(("obs", "src"), None, None),
        P(("obs", "src"), None, None),
        P(("obs", "src"), None, None),
        P(None, "obs", None, "src", None),
        P("obs", None, "src", None),
    )
    return jax.shard_map(
        functools.partial(per_device, mesh.shape["obs"], mesh.shape["src"]),
        mesh=mesh,
        in_specs=placed,
        out_specs=P(None, ("obs", "src"), None, None),
        check_vma=False,
    )
```

```python
import contextlib
import functools

import jax
import jax.numpy as jnp
from jax import lax
from jax.experimental import pallas as pl
from jax.experimental.pallas import tpu as pltpu
from jax.sharding import PartitionSpec as P

MESH = pl.DeviceIdType.MESH
F32 = jnp.float32
BF16 = jnp.bfloat16
NT = (((1,), (1,)), ((), ()))
VMEM_LIMIT = 60000 * 1024


def scope(name):
    return contextlib.nullcontext()


def flipped(me, bits, count):
    other = me
    place = 1
    while place < count:
        if bits & place:
            other = other + (1 - 2 * ((me // place) % 2)) * place
        place *= 2
    return other


def partner(me, turn, count):
    if count & (count - 1) == 0:
        return flipped(me, count - turn, count)
    return lax.rem(me + turn, count)


def sender(me, turn, count):
    if count & (count - 1) == 0:
        return partner(me, turn, count)
    return lax.rem(me + count - turn, count)


def farthest_first(me, count):
    upper = (2 * me) // count
    sign = 1 - 2 * upper
    near_end = me * (1 - upper) + (count - 1 - me) * upper
    peers = []
    for i in range(count - 1):
        one_sided = (3 * count - 2 - i - 2 * near_end) // (2 * count)
        left = count - 2 - i
        paired = (left // 2 + 1) * (2 * (left % 2) - 1)
        peers.append(me + sign * (one_sided * (count - 1 - near_end - i) + (1 - one_sided) * paired))
    return peers


def kernel(n_obs, n_src, hist_ref, inc_ref, proj_ref, expand_ref, near_ref, coup_ref, lags_ref,
           out_ref, last_ref, xn, yl,
           lag_ref, hv, av, pv, nv, cv, cf, wv, yv, bv, mv, qh, qn, sendp, recvp, base,
           l_sem, hs_sem, hr_sem, hf_sem, qr_sem, ps_sem, pr_sem):
    o = lax.axis_index("obs")
    s = lax.axis_index("src")
    hist, clusters, excite, unknowns = hist_ref.shape
    steps = inc_ref.shape[0]
    rank = proj_ref.shape[1]
    width = clusters * rank
    sources = lag_ref.shape[2]
    tile = 512
    tiles = unknowns // tile
    pairs = n_src // 2
    deep = 2 * width

    soon = min(2, steps)
    early = (soon + 1) * excite

    def place(step):
        return step if step < soon else step + 1

    def rows(index, size):
        return pl.ds(index * size, size)

    def cols(index, size):
        return slice(index * size, (index + 1) * size)

    def local(src, dst, sem):
        pltpu.make_async_copy(src, dst, sem).start()

    def landed(ref, sem):
        pltpu.make_async_copy(ref, ref, sem).wait()

    for c in range(clusters):
        local(proj_ref.at[c], pv.at[c, rows(c, rank)], l_sem.at[0])
    for k in range(hist):
        for c in range(clusters):
            local(hist_ref.at[k, c], hv.at[k, c], l_sem.at[1 + k])

    mine = s % 2
    own = s // 2
    sibling = s + 1 - 2 * mine
    others = [partner(own, turn, pairs) for turn in range(1, pairs)]
    arriving = [sender(own, turn, pairs) for turn in range(pairs - 1, 0, -1)]
    q_peers = [pair * 2 + core for pair in others for core in range(2)] + [sibling]
    p_peers = farthest_first(o, n_obs)

    barrier = pltpu.get_barrier_semaphore()
    for peer in q_peers:
        pl.semaphore_signal(barrier, inc=1, device_id=(o, peer), device_id_type=MESH)
    for peer in p_peers:
        pl.semaphore_signal(barrier, inc=1, device_id=(peer, s), device_id_type=MESH)

    local(lags_ref, lag_ref, l_sem.at[hist + 1])
    quarter = coup_ref.shape[1] // 4
    for p in range(coup_ref.shape[0]):
        for part in range(4):
            local(coup_ref.at[p, rows(part, quarter)], cv.at[p, rows(part, quarter)], l_sem.at[hist + 2])


    def stack_sem(c):
        return l_sem.at[0] if c == 0 else l_sem.at[hist - 1 + 2 * c]

    def near_sem(c, j):
        return l_sem.at[1 + j] if c == 0 else l_sem.at[hist + 2 * c]

    late_sem = l_sem.at[hist + 1 + 2 * max(1, clusters - 1)]

    def stack_loads(c, part):
        for t in range(soon) if part == 0 else range(soon, steps):
            local(inc_ref.at[t, c], av.at[c, rows(place(t), excite)], stack_sem(c) if part == 0 else late_sem)
        if part == 0:
            local(expand_ref.at[c], av.at[c, rows(soon, excite)], stack_sem(c))

    def near_load(c, j):
        local(near_ref.at[c, :, cols(j, tile)], nv.at[c, :, cols(j, tile)], near_sem(c, j))

    def remote(src, dst, send_sem, recv_sem, device):
        return pltpu.make_async_remote_copy(
            src_ref=src, dst_ref=dst, send_sem=send_sem, recv_sem=recv_sem, device_id=device, device_id_type=MESH)

    def arrived(ref, sem):
        remote(ref, ref, hs_sem.at[0], sem, (o, sibling)).wait_recv()

    def sent(ref, sem):
        remote(ref, ref, sem, hr_sem.at[0], (o, sibling)).wait_send()

    for k in range(hist):
        with scope("hload"):
            if k == 0:
                landed(proj_ref, l_sem.at[0])
            landed(hv.at[k], l_sem.at[1 + k])
        with scope("project"):
            qh[s, k] = jnp.concatenate([
                lax.dot_general(hv[k, c], pv[c, cols(c, rank)], NT, preferred_element_type=F32)
                for c in range(clusters)], axis=1).astype(BF16)
        if k == 0:
            with scope("barrier"):
                pl.semaphore_wait(barrier, n_src + n_obs - 2)
        for pair in others:
            remote(qh.at[s, k], qh.at[s, k], hs_sem.at[0], hr_sem.at[k], (o, pair * 2 + mine)).start()
        remote(qh.at[s, k], qh.at[s, k], hs_sem.at[0], hf_sem.at[k], (o, sibling)).start()
        if k == 0:
            stack_loads(0, 0)
            near_load(0, 0)
    for j in range(1, tiles):
        near_load(0, j)
    for c in range(clusters):
        for k in range(clusters):
            if k != c:
                pv[c, cols(k, rank)] = jnp.zeros((rank, unknowns), BF16)
                xn[c, cols(k, rank)] = jnp.zeros((rank, unknowns), BF16)

    with scope("cload"):
        landed(lag_ref, l_sem.at[hist + 1])
        landed(coup_ref, l_sem.at[hist + 2])
    for c in range(1, clusters):
        stack_loads(c, 0)
        for j in range(tiles):
            near_load(c, j)
    for c in range(clusters):
        stack_loads(c, 1)
    lane = lax.broadcasted_iota(jnp.int32, (rank, width), 1)

    def build(j, carry):
        for p in range(2):
            cf[p] = cv[p, pl.ds(pl.multiple_of(j * (rank * n_obs), rank * n_obs), rank * n_obs), :].astype(F32)
        at = pl.ds(pl.multiple_of(j * rank, rank), rank)
        for to in range(n_obs):
            lag = jnp.full((rank, width), lag_ref[to, 0, j], jnp.int32)
            for k in range(1, clusters):
                lag = jnp.where(lane >= k * rank, lag_ref[to, k, j], lag)
            first = cf[0, pl.ds(to, rank, stride=n_obs), :]
            second = cf[1, pl.ds(to, rank, stride=n_obs), :]
            zero = jnp.zeros_like(first)
            one, two = lag == 1, lag == 2
            wv[0, at, cols(to, width)] = jnp.where(one, first, zero).astype(BF16)
            wv[1, at, cols(to, width)] = jnp.where(two, first, jnp.where(one, second, zero)).astype(BF16)
            wv[2, at, cols(to, width)] = jnp.where(two, second, zero).astype(BF16)
        return carry

    with scope("build"):
        lax.fori_loop(0, sources, build, 0)

    def near_tile(c, j, part):
        at = cols(j, tile)
        if part == 0:
            if j == 0:
                landed(av.at[c, :early], stack_sem(c))
            if c == 0:
                landed(nv.at[c, :, at], near_sem(c, j))
            elif j == 0:
                landed(nv.at[c], near_sem(c, j))
            value = jnp.dot(av[c, :early], nv[c, :, at], preferred_element_type=F32)
            yv[c, :early, at] = value
            xn[c, cols(c, rank), at] = value[soon * excite:].astype(BF16)
        else:
            if c == 0 and j == 0:
                landed(av.at[:, early:], late_sem)
            value = jnp.dot(av[c, early:], nv[c, :, at], preferred_element_type=F32)
            yv[c, early:, at] = value
            yl[c, :, at] = value[value.shape[0] - excite:]

    def near_end(c, part):
        which = slice(early) if part == 0 else slice(early, (steps + 1) * excite)
        value = lax.dot_general(yv[c, which].astype(BF16), pv[c], NT, preferred_element_type=F32)
        keep = slice(soon * excite) if part == 0 else slice(soon * excite, steps * excite)
        made = value[:soon * excite] if part == 0 else value
        if c == 0:
            bv[keep] = made
        else:
            bv[keep] += made
        if part == 0:
            mv[cols(c, rank)] = value[soon * excite:].astype(BF16)

    def near(c, part, chosen):
        for j in chosen:
            with scope(f"near{c}_{part}_{j}"):
                near_tile(c, j, part)
        if tiles - 1 in chosen:
            with scope(f"nearend{c}_{part}"):
                near_end(c, part)

    def rows_of(pair):
        return pl.ds(pl.multiple_of(pair * deep, deep), deep)

    def both(get, pair):
        return jnp.concatenate([get(pair * 2 + core) for core in range(2)], axis=1)

    def p_sem(step):
        return hr_sem.at[0] if step % 2 else pr_sem.at[0]

    def q_sem(step, group):
        return hf_sem.at[group] if step % 2 else qr_sem.at[group]

    def send_partial(step, total):
        for to in range(n_obs):
            sendp[step * n_obs + to] = total[:, cols(to, width)].astype(BF16)
        for peer in p_peers:
            remote(sendp.at[step * n_obs + peer], recvp.at[step * n_obs + o], ps_sem.at[0], p_sem(step),
                   (peer, s)).start()

    def slot_of(k):
        return jnp.concatenate([qh[j, k] for j in range(n_src)], axis=1)

    def forward(k):
        with scope("forward"):
            arrived(qh.at[pl.ds(0, pairs - 1), k], hr_sem.at[k])
            for pair in arriving:
                slot = pair * 2 + mine
                remote(qh.at[slot, k], qh.at[slot, k], hs_sem.at[0], hf_sem.at[k], (o, sibling)).start()

    def first(k):
        with scope("hwait"):
            arrived(qh.at[pl.ds(0, pairs), k], hf_sem.at[k])
        with scope("first"):
            term = jnp.dot(slot_of(k), wv[hist - 1 - k], preferred_element_type=F32)
            base[0] = term if k == 0 else base[0] + term

    for j in range(tiles):
        with scope(f"near0_0_{j}"):
            near_tile(0, j, 0)
    for k in range(hist):
        forward(k)
    for k in range(hist - 1):
        first(k)
    with scope("hwait"):
        arrived(qh.at[pl.ds(0, pairs), hist - 1], hf_sem.at[hist - 1])
    with scope("sendp"):
        term = jnp.dot(slot_of(hist - 1), wv[0], preferred_element_type=F32)
        send_partial(0, base[0] + term)

    with scope("nearend0_0"):
        near_end(0, 0)
    for c in range(1, clusters):
        near(c, 0, range(tiles))

    sent(qh.at[pl.ds(0, n_src - 1)], hs_sem.at[0])
    pending = [(c, 1, range(j, j + 1)) for c in range(clusters) for j in range(tiles)]
    shares = max(1, 2 * (soon - 1) + 2)
    share = -(-len(pending) // shares)

    def later(window):
        for c, part, chosen in pending[window * share:(window + 1) * share]:
            near(c, part, chosen)

    def newest_term(step):
        total = base[step + 1]
        for turn, pair in enumerate([own] + arriving):
            with scope(f"waitq{step}"):
                if turn == 0:
                    arrived(qn.at[step * n_src + sibling], q_sem(step, 0))
                elif turn == 1 and pairs > 2:
                    arrived(qn.at[pl.ds(step * n_src, 2 * (pairs - 2))], q_sem(step, 1))
                elif turn == pairs - 1:
                    arrived(qn.at[pl.ds(step * n_src + pair * 2, 2)], q_sem(step, 2))
            part = both(lambda slot: qn[step * n_src + slot], pair)
            total = total + jnp.dot(part, wv[0, rows_of(pair), :], preferred_element_type=F32)
        return total

    def older_terms():
        with scope("hbase"):
            for ahead in range(1, hist):
                total = None
                for d in range(ahead + 1, hist + 1):
                    term = jnp.dot(slot_of(hist + ahead - d), wv[d - 1], preferred_element_type=F32)
                    total = term if total is None else total + term
                base[ahead] = total
            for ahead in range(hist, steps):
                base[ahead] = jnp.zeros((excite, n_obs * width), F32)

    def finish(step, field):
        for c in range(clusters):
            far = jnp.dot(field, xn[c], preferred_element_type=F32)
            out_ref[step, c] = (yv[c, cols(place(step), excite)] - far).astype(BF16)

    for step in range(steps):
        field = sendp[step * n_obs + o].astype(F32)
        with scope(f"waitp{step}"):
            arrived(recvp.at[pl.ds(0, n_obs - 1)], p_sem(step))
        for peer in p_peers:
            field = field + recvp[step * n_obs + peer].astype(F32)
        field = field.astype(BF16)
        if step + 1 == steps:
            last_ref[...] = field
            break
        newest = bv[cols(step, excite)] - jnp.dot(field, mv[...], preferred_element_type=F32)
        qn[step * n_src + s] = newest.astype(BF16)
        for turn, peer in enumerate(q_peers):
            group = 2 if turn < 2 else 1 if peer is not sibling else 0
            remote(qn.at[step * n_src + s], qn.at[step * n_src + s], hs_sem.at[0], q_sem(step, group),
                   (o, peer)).start()
        with scope(f"finish{step}"):
            finish(step, field)
        if step == 0:
            older_terms()
        later(2 * step)
        with scope(f"newest{step}"):
            total = newest_term(step)
        send_partial(step + 1, total)
        with scope(f"base{step}"):
            columns = jnp.concatenate([qn[step * n_src + j] for j in range(n_src)], axis=1)
            for d in range(2, hist + 1):
                if step + d < steps:
                    base[step + d] += jnp.dot(columns, wv[d - 1], preferred_element_type=F32)
        later(2 * step + 1)

    with scope("sent"):
        sent(qn.at[pl.ds(0, (steps - 1) * (n_src - 1))], hs_sem.at[0])
        sent(sendp.at[pl.ds(0, steps * (n_obs - 1))], ps_sem.at[0])


def hand_on(made_ref, last_ref, x_ref, y_ref, out_ref, held, sem):
    steps, clusters = out_ref.shape[:2]
    for t in range(steps - 1):
        pltpu.make_async_copy(made_ref.at[t], out_ref.at[t], sem.at[0]).start()
    for c in range(clusters):
        far = jnp.dot(last_ref[...], x_ref[c], preferred_element_type=F32)
        held[c] = (y_ref[c] - far).astype(BF16)
        pltpu.make_async_copy(held.at[c], out_ref.at[steps - 1, c], sem.at[0]).start()
    pltpu.make_async_copy(out_ref, out_ref, sem.at[0]).wait()


def per_device(n_obs, n_src, history, incident, proj_basis, expand_basis, near_inverse, couplings, lags):
    hist, clusters, excite, unknowns = history.shape
    steps = incident.shape[0]
    rank = proj_basis.shape[1]
    width = clusters * rank
    taps, src_rows = couplings.shape[:2]
    sources = lags.shape[0]
    obs_cols = n_obs * width
    pairs = n_src // 2
    flat = couplings.reshape(taps, src_rows * n_obs, width)
    lag_table = jnp.transpose(lags.reshape(sources, n_obs, clusters), (1, 2, 0))
    stacked = (steps + 1) * excite
    any_spec = pl.BlockSpec(memory_space=pl.ANY)
    vmem_spec = pl.BlockSpec(memory_space=pltpu.VMEM)
    dma = pltpu.SemaphoreType.DMA
    made = pl.pallas_call(
        functools.partial(kernel, n_obs, n_src),
        out_shape=(
            pltpu.VMEM((steps - 1, *incident.shape[1:]), BF16),
            pltpu.VMEM((excite, width), BF16),
            pltpu.VMEM((clusters, width, unknowns), BF16),
            pltpu.VMEM((clusters, excite, unknowns), F32),
        ),
        in_specs=[any_spec] * 7,
        out_specs=(vmem_spec,) * 4,
        scratch_shapes=[
            pltpu.SMEM((n_obs, clusters, sources), jnp.int32),
            pltpu.VMEM((hist, clusters, excite, unknowns), BF16),
            pltpu.VMEM((clusters, stacked, unknowns), BF16),
            pltpu.VMEM((clusters, width, unknowns), BF16),
            pltpu.VMEM((clusters, unknowns, unknowns), BF16),
            pltpu.VMEM((taps, src_rows * n_obs, width), BF16),
            pltpu.VMEM((taps, rank * n_obs, width), F32),
            pltpu.VMEM((hist, src_rows, obs_cols), BF16),
            pltpu.VMEM((clusters, stacked, unknowns), F32),
            pltpu.VMEM((steps * excite, width), F32),
            pltpu.VMEM((width, width), BF16),
            pltpu.VMEM((n_src, hist, excite, width), BF16),
            pltpu.VMEM(((steps - 1) * n_src, excite, width), BF16),
            pltpu.VMEM((steps * n_obs, excite, width), BF16),
            pltpu.VMEM((steps * n_obs, excite, width), BF16),
            pltpu.VMEM((steps, excite, obs_cols), F32),
            dma((hist + 2 + 2 * max(1, clusters - 1),)),
            dma((1,)),
            dma((hist,)),
            dma((max(hist, 3),)),
            dma((3,)),
            dma((1,)),
            dma((1,)),
        ],
        compiler_params=pltpu.CompilerParams(
            collective_id=0, has_side_effects=True, vmem_limit_bytes=VMEM_LIMIT
        ),
    )(history, incident, proj_basis, expand_basis, near_inverse, flat, lag_table)
    return pl.pallas_call(
        hand_on,
        out_shape=jax.ShapeDtypeStruct(incident.shape, BF16),
        in_specs=[vmem_spec] * 4,
        out_specs=any_spec,
        scratch_shapes=[pltpu.VMEM((clusters, excite, unknowns), BF16), dma((1,))],
        compiler_params=pltpu.CompilerParams(vmem_limit_bytes=8000 * 1024),
    )(*made)


def solution(mesh):
    placed = (
        P(None, ("obs", "src"), None, None),
        P(None, ("obs", "src"), None, None),
        P(("obs", "src"), None, None),
        P(("obs", "src"), None, None),
        P(("obs", "src"), None, None),
        P(None, "obs", None, "src", None),
        P("obs", None, "src", None),
    )
    return jax.shard_map(
        functools.partial(per_device, mesh.shape["obs"], mesh.shape["src"]),
        mesh=mesh,
        in_specs=placed,
        out_specs=P(None, ("obs", "src"), None, None),
        check_vma=False,
    )
```

```python
import contextlib
import functools

import jax
import jax.numpy as jnp
from jax import lax
from jax.experimental import pallas as pl
from jax.experimental.pallas import tpu as pltpu
from jax.sharding import PartitionSpec as P

MESH = pl.DeviceIdType.MESH
F32 = jnp.float32
BF16 = jnp.bfloat16
NT = (((1,), (1,)), ((), ()))
VMEM_LIMIT = 60000 * 1024


def scope(name):
    return contextlib.nullcontext()


def flipped(me, bits, count):
    other = me
    place = 1
    while place < count:
        if bits & place:
            other = other + (1 - 2 * ((me // place) % 2)) * place
        place *= 2
    return other


def partner(me, turn, count):
    if count & (count - 1) == 0:
        return flipped(me, count - turn, count)
    return lax.rem(me + turn, count)


def sender(me, turn, count):
    if count & (count - 1) == 0:
        return partner(me, turn, count)
    return lax.rem(me + count - turn, count)


def farthest_first(me, count):
    upper = (2 * me) // count
    sign = 1 - 2 * upper
    near_end = me * (1 - upper) + (count - 1 - me) * upper
    peers = []
    for i in range(count - 1):
        one_sided = (3 * count - 2 - i - 2 * near_end) // (2 * count)
        left = count - 2 - i
        paired = (left // 2 + 1) * (2 * (left % 2) - 1)
        peers.append(me + sign * (one_sided * (count - 1 - near_end - i) + (1 - one_sided) * paired))
    return peers


def kernel(n_obs, n_src, hist_ref, inc_ref, proj_ref, expand_ref, near_ref, coup_ref, lags_ref,
           out_ref, last_ref, xn, yl,
           lag_ref, hv, av, pv, nv, cv, cf, wv, yv, bv, mv, qh, qn, sendp, recvp, base,
           l_sem, hs_sem, hr_sem, hf_sem, qr_sem, ps_sem, pr_sem):
    o = lax.axis_index("obs")
    s = lax.axis_index("src")
    hist, clusters, excite, unknowns = hist_ref.shape
    steps = inc_ref.shape[0]
    rank = proj_ref.shape[1]
    width = clusters * rank
    sources = lag_ref.shape[2]
    tile = 512
    tiles = unknowns // tile
    pairs = n_src // 2
    deep = 2 * width

    soon = min(2, steps)
    early = (soon + 1) * excite

    def place(step):
        return step if step < soon else step + 1

    def rows(index, size):
        return pl.ds(index * size, size)

    def cols(index, size):
        return slice(index * size, (index + 1) * size)

    def local(src, dst, sem):
        pltpu.make_async_copy(src, dst, sem).start()

    def landed(ref, sem):
        pltpu.make_async_copy(ref, ref, sem).wait()

    for part in range(2):
        for c in range(clusters):
            local(proj_ref.at[c, rows(part, rank // 2)], pv.at[c, rows(2 * c + part, rank // 2)], l_sem.at[0])
            local(hist_ref.at[0, c, rows(part, excite // 2)], hv.at[0, c, rows(part, excite // 2)], l_sem.at[1])
    for k in range(1, hist):
        for c in range(clusters):
            local(hist_ref.at[k, c], hv.at[k, c], l_sem.at[1 + k])

    mine = s % 2
    own = s // 2
    sibling = s + 1 - 2 * mine
    others = [partner(own, turn, pairs) for turn in range(1, pairs)]
    arriving = [sender(own, turn, pairs) for turn in range(pairs - 1, 0, -1)]
    q_peers = [pair * 2 + core for pair in others for core in range(2)] + [sibling]
    p_peers = farthest_first(o, n_obs)

    barrier = pltpu.get_barrier_semaphore()
    for peer in q_peers:
        pl.semaphore_signal(barrier, inc=1, device_id=(o, peer), device_id_type=MESH)
    for peer in p_peers:
        pl.semaphore_signal(barrier, inc=1, device_id=(peer, s), device_id_type=MESH)

    local(lags_ref, lag_ref, l_sem.at[hist + 1])
    quarter = coup_ref.shape[1] // 4
    for p in range(coup_ref.shape[0]):
        for part in range(4):
            local(coup_ref.at[p, rows(part, quarter)], cv.at[p, rows(part, quarter)], l_sem.at[hist + 2])


    def stack_sem(c):
        return l_sem.at[0] if c == 0 else l_sem.at[hist - 1 + 2 * c]

    def near_sem(c, j):
        return l_sem.at[1 + j] if c == 0 else l_sem.at[hist + 2 * c]

    late_sem = l_sem.at[hist + 1 + 2 * max(1, clusters - 1)]

    def stack_loads(c, part):
        for t in range(soon) if part == 0 else range(soon, steps):
            local(inc_ref.at[t, c], av.at[c, rows(place(t), excite)], stack_sem(c) if part == 0 else late_sem)
        if part == 0:
            local(expand_ref.at[c], av.at[c, rows(soon, excite)], stack_sem(c))

    def near_load(c, j):
        local(near_ref.at[c, :, cols(j, tile)], nv.at[c, :, cols(j, tile)], near_sem(c, j))

    def remote(src, dst, send_sem, recv_sem, device):
        return pltpu.make_async_remote_copy(
            src_ref=src, dst_ref=dst, send_sem=send_sem, recv_sem=recv_sem, device_id=device, device_id_type=MESH)

    def arrived(ref, sem):
        remote(ref, ref, hs_sem.at[0], sem, (o, sibling)).wait_recv()

    def sent(ref, sem):
        remote(ref, ref, sem, hr_sem.at[0], (o, sibling)).wait_send()

    for k in range(hist):
        with scope("hload"):
            if k == 0:
                landed(proj_ref, l_sem.at[0])
            landed(hv.at[k], l_sem.at[1 + k])
        with scope("project"):
            qh[s, k] = jnp.concatenate([
                lax.dot_general(hv[k, c], pv[c, cols(c, rank)], NT, preferred_element_type=F32)
                for c in range(clusters)], axis=1).astype(BF16)
        if k == 0:
            with scope("barrier"):
                pl.semaphore_wait(barrier, n_src + n_obs - 2)
        for pair in others:
            remote(qh.at[s, k], qh.at[s, k], hs_sem.at[0], hr_sem.at[k], (o, pair * 2 + mine)).start()
        remote(qh.at[s, k], qh.at[s, k], hs_sem.at[0], hf_sem.at[k], (o, sibling)).start()
        if k == 0:
            stack_loads(0, 0)
            near_load(0, 0)
    for j in range(1, tiles):
        near_load(0, j)
    for c in range(clusters):
        for k in range(clusters):
            if k != c:
                pv[c, cols(k, rank)] = jnp.zeros((rank, unknowns), BF16)
                xn[c, cols(k, rank)] = jnp.zeros((rank, unknowns), BF16)

    with scope("cload"):
        landed(lag_ref, l_sem.at[hist + 1])
        landed(coup_ref, l_sem.at[hist + 2])
    for c in range(1, clusters):
        stack_loads(c, 0)
        for j in range(tiles):
            near_load(c, j)
    for c in range(clusters):
        stack_loads(c, 1)
    lane = lax.broadcasted_iota(jnp.int32, (rank, width), 1)

    def build(j, carry):
        for p in range(2):
            cf[p] = cv[p, pl.ds(pl.multiple_of(j * (rank * n_obs), rank * n_obs), rank * n_obs), :].astype(F32)
        at = pl.ds(pl.multiple_of(j * rank, rank), rank)
        for to in range(n_obs):
            lag = jnp.full((rank, width), lag_ref[to, 0, j], jnp.int32)
            for k in range(1, clusters):
                lag = jnp.where(lane >= k * rank, lag_ref[to, k, j], lag)
            first = cf[0, pl.ds(to, rank, stride=n_obs), :]
            second = cf[1, pl.ds(to, rank, stride=n_obs), :]
            zero = jnp.zeros_like(first)
            one, two = lag == 1, lag == 2
            wv[0, at, cols(to, width)] = jnp.where(one, first, zero).astype(BF16)
            wv[1, at, cols(to, width)] = jnp.where(two, first, jnp.where(one, second, zero)).astype(BF16)
            wv[2, at, cols(to, width)] = jnp.where(two, second, zero).astype(BF16)
        return carry

    with scope("build"):
        lax.fori_loop(0, sources, build, 0)

    def near_tile(c, j, part):
        at = cols(j, tile)
        if part == 0:
            if j == 0:
                landed(av.at[c, :early], stack_sem(c))
            if c == 0:
                landed(nv.at[c, :, at], near_sem(c, j))
            elif j == 0:
                landed(nv.at[c], near_sem(c, j))
            value = jnp.dot(av[c, :early], nv[c, :, at], preferred_element_type=F32)
            yv[c, :early, at] = value
            xn[c, cols(c, rank), at] = value[soon * excite:].astype(BF16)
        else:
            if c == 0 and j == 0:
                landed(av.at[:, early:], late_sem)
            value = jnp.dot(av[c, early:], nv[c, :, at], preferred_element_type=F32)
            yv[c, early:, at] = value
            yl[c, :, at] = value[value.shape[0] - excite:]

    def near_end(c, part):
        which = slice(early) if part == 0 else slice(early, (steps + 1) * excite)
        value = lax.dot_general(yv[c, which].astype(BF16), pv[c], NT, preferred_element_type=F32)
        keep = slice(soon * excite) if part == 0 else slice(soon * excite, steps * excite)
        made = value[:soon * excite] if part == 0 else value
        if c == 0:
            bv[keep] = made
        else:
            bv[keep] += made
        if part == 0:
            mv[cols(c, rank)] = value[soon * excite:].astype(BF16)

    def near(c, part, chosen):
        for j in chosen:
            with scope(f"near{c}_{part}_{j}"):
                near_tile(c, j, part)
        if tiles - 1 in chosen:
            with scope(f"nearend{c}_{part}"):
                near_end(c, part)

    def rows_of(pair):
        return pl.ds(pl.multiple_of(pair * deep, deep), deep)

    def both(get, pair):
        return jnp.concatenate([get(pair * 2 + core) for core in range(2)], axis=1)

    def p_sem(step):
        return hr_sem.at[0] if step % 2 else pr_sem.at[0]

    def q_sem(step, group):
        return hf_sem.at[group] if step % 2 else qr_sem.at[group]

    def send_partial(step, total):
        for to in range(n_obs):
            sendp[step * n_obs + to] = total[:, cols(to, width)].astype(BF16)
        for peer in p_peers:
            remote(sendp.at[step * n_obs + peer], recvp.at[step * n_obs + o], ps_sem.at[0], p_sem(step),
                   (peer, s)).start()

    def slot_of(k):
        return jnp.concatenate([qh[j, k] for j in range(n_src)], axis=1)

    def forward(k):
        with scope("forward"):
            arrived(qh.at[pl.ds(0, pairs - 1), k], hr_sem.at[k])
            for pair in arriving:
                slot = pair * 2 + mine
                remote(qh.at[slot, k], qh.at[slot, k], hs_sem.at[0], hf_sem.at[k], (o, sibling)).start()

    def first(k):
        with scope("hwait"):
            arrived(qh.at[pl.ds(0, pairs), k], hf_sem.at[k])
        with scope("first"):
            term = jnp.dot(slot_of(k), wv[hist - 1 - k], preferred_element_type=F32)
            base[0] = term if k == 0 else base[0] + term

    for j in range(tiles):
        with scope(f"near0_0_{j}"):
            near_tile(0, j, 0)
    for k in range(hist):
        forward(k)
    for k in range(hist - 1):
        first(k)
    with scope("hwait"):
        arrived(qh.at[pl.ds(0, pairs), hist - 1], hf_sem.at[hist - 1])
    with scope("sendp"):
        term = jnp.dot(slot_of(hist - 1), wv[0], preferred_element_type=F32)
        send_partial(0, base[0] + term)

    with scope("nearend0_0"):
        near_end(0, 0)
    for c in range(1, clusters):
        near(c, 0, range(tiles))

    sent(qh.at[pl.ds(0, n_src - 1)], hs_sem.at[0])
    pending = [(c, 1, range(j, j + 1)) for c in range(clusters) for j in range(tiles)]
    shares = max(1, 2 * (soon - 1) + 2)
    share = -(-len(pending) // shares)

    def later(window):
        for c, part, chosen in pending[window * share:(window + 1) * share]:
            near(c, part, chosen)

    def newest_term(step):
        total = base[step + 1]
        for turn, pair in enumerate([own] + arriving):
            with scope(f"waitq{step}"):
                if turn == 0:
                    arrived(qn.at[step * n_src + sibling], q_sem(step, 0))
                elif turn == 1 and pairs > 2:
                    arrived(qn.at[pl.ds(step * n_src, 2 * (pairs - 2))], q_sem(step, 1))
                elif turn == pairs - 1:
                    arrived(qn.at[pl.ds(step * n_src + pair * 2, 2)], q_sem(step, 2))
            part = both(lambda slot: qn[step * n_src + slot], pair)
            total = total + jnp.dot(part, wv[0, rows_of(pair), :], preferred_element_type=F32)
        return total

    def older_terms():
        with scope("hbase"):
            for ahead in range(1, hist):
                total = None
                for d in range(ahead + 1, hist + 1):
                    term = jnp.dot(slot_of(hist + ahead - d), wv[d - 1], preferred_element_type=F32)
                    total = term if total is None else total + term
                base[ahead] = total
            for ahead in range(hist, steps):
                base[ahead] = jnp.zeros((excite, n_obs * width), F32)

    def finish(step, field):
        for c in range(clusters):
            far = jnp.dot(field, xn[c], preferred_element_type=F32)
            out_ref[step, c] = (yv[c, cols(place(step), excite)] - far).astype(BF16)

    for step in range(steps):
        field = sendp[step * n_obs + o].astype(F32)
        with scope(f"waitp{step}"):
            arrived(recvp.at[pl.ds(0, n_obs - 1)], p_sem(step))
        for peer in p_peers:
            field = field + recvp[step * n_obs + peer].astype(F32)
        field = field.astype(BF16)
        if step + 1 == steps:
            last_ref[...] = field
            break
        newest = bv[cols(step, excite)] - jnp.dot(field, mv[...], preferred_element_type=F32)
        qn[step * n_src + s] = newest.astype(BF16)
        for turn, peer in enumerate(q_peers):
            group = 2 if turn < 2 else 1 if peer is not sibling else 0
            remote(qn.at[step * n_src + s], qn.at[step * n_src + s], hs_sem.at[0], q_sem(step, group),
                   (o, peer)).start()
        with scope(f"finish{step}"):
            finish(step, field)
        if step == 0:
            older_terms()
        later(2 * step)
        with scope(f"newest{step}"):
            total = newest_term(step)
        send_partial(step + 1, total)
        with scope(f"base{step}"):
            columns = jnp.concatenate([qn[step * n_src + j] for j in range(n_src)], axis=1)
            for d in range(2, hist + 1):
                if step + d < steps:
                    base[step + d] += jnp.dot(columns, wv[d - 1], preferred_element_type=F32)
        later(2 * step + 1)

    with scope("sent"):
        sent(qn.at[pl.ds(0, (steps - 1) * (n_src - 1))], hs_sem.at[0])
        sent(sendp.at[pl.ds(0, steps * (n_obs - 1))], ps_sem.at[0])


def hand_on(made_ref, last_ref, x_ref, y_ref, out_ref, held, sem):
    steps, clusters = out_ref.shape[:2]
    for t in range(steps - 1):
        pltpu.make_async_copy(made_ref.at[t], out_ref.at[t], sem.at[0]).start()
    for c in range(clusters):
        far = jnp.dot(last_ref[...], x_ref[c], preferred_element_type=F32)
        held[c] = (y_ref[c] - far).astype(BF16)
        pltpu.make_async_copy(held.at[c], out_ref.at[steps - 1, c], sem.at[0]).start()
    pltpu.make_async_copy(out_ref, out_ref, sem.at[0]).wait()


def per_device(n_obs, n_src, history, incident, proj_basis, expand_basis, near_inverse, couplings, lags):
    hist, clusters, excite, unknowns = history.shape
    steps = incident.shape[0]
    rank = proj_basis.shape[1]
    width = clusters * rank
    taps, src_rows = couplings.shape[:2]
    sources = lags.shape[0]
    obs_cols = n_obs * width
    pairs = n_src // 2
    flat = couplings.reshape(taps, src_rows * n_obs, width)
    lag_table = jnp.transpose(lags.reshape(sources, n_obs, clusters), (1, 2, 0))
    stacked = (steps + 1) * excite
    any_spec = pl.BlockSpec(memory_space=pl.ANY)
    vmem_spec = pl.BlockSpec(memory_space=pltpu.VMEM)
    dma = pltpu.SemaphoreType.DMA
    made = pl.pallas_call(
        functools.partial(kernel, n_obs, n_src),
        out_shape=(
            pltpu.VMEM((steps - 1, *incident.shape[1:]), BF16),
            pltpu.VMEM((excite, width), BF16),
            pltpu.VMEM((clusters, width, unknowns), BF16),
            pltpu.VMEM((clusters, excite, unknowns), F32),
        ),
        in_specs=[any_spec] * 7,
        out_specs=(vmem_spec,) * 4,
        scratch_shapes=[
            pltpu.SMEM((n_obs, clusters, sources), jnp.int32),
            pltpu.VMEM((hist, clusters, excite, unknowns), BF16),
            pltpu.VMEM((clusters, stacked, unknowns), BF16),
            pltpu.VMEM((clusters, width, unknowns), BF16),
            pltpu.VMEM((clusters, unknowns, unknowns), BF16),
            pltpu.VMEM((taps, src_rows * n_obs, width), BF16),
            pltpu.VMEM((taps, rank * n_obs, width), F32),
            pltpu.VMEM((hist, src_rows, obs_cols), BF16),
            pltpu.VMEM((clusters, stacked, unknowns), F32),
            pltpu.VMEM((steps * excite, width), F32),
            pltpu.VMEM((width, width), BF16),
            pltpu.VMEM((n_src, hist, excite, width), BF16),
            pltpu.VMEM(((steps - 1) * n_src, excite, width), BF16),
            pltpu.VMEM((steps * n_obs, excite, width), BF16),
            pltpu.VMEM((steps * n_obs, excite, width), BF16),
            pltpu.VMEM((steps, excite, obs_cols), F32),
            dma((hist + 2 + 2 * max(1, clusters - 1),)),
            dma((1,)),
            dma((hist,)),
            dma((max(hist, 3),)),
            dma((3,)),
            dma((1,)),
            dma((1,)),
        ],
        compiler_params=pltpu.CompilerParams(
            collective_id=0, has_side_effects=True, vmem_limit_bytes=VMEM_LIMIT
        ),
    )(history, incident, proj_basis, expand_basis, near_inverse, flat, lag_table)
    return pl.pallas_call(
        hand_on,
        out_shape=jax.ShapeDtypeStruct(incident.shape, BF16),
        in_specs=[vmem_spec] * 4,
        out_specs=any_spec,
        scratch_shapes=[pltpu.VMEM((clusters, excite, unknowns), BF16), dma((1,))],
        compiler_params=pltpu.CompilerParams(vmem_limit_bytes=8000 * 1024),
    )(*made)


def solution(mesh):
    placed = (
        P(None, ("obs", "src"), None, None),
        P(None, ("obs", "src"), None, None),
        P(("obs", "src"), None, None),
        P(("obs", "src"), None, None),
        P(("obs", "src"), None, None),
        P(None, "obs", None, "src", None),
        P("obs", None, "src", None),
    )
    return jax.shard_map(
        functools.partial(per_device, mesh.shape["obs"], mesh.shape["src"]),
        mesh=mesh,
        in_specs=placed,
        out_specs=P(None, ("obs", "src"), None, None),
        check_vma=False,
    )
```
